32 devices in a mesh: seq: 8 (over z, x), head: 4 (over y, core).
Axes of the slice: x: 2, y: 2, z: 4, core: 2. Of those that a mesh axis runs over, the one named last changes fastest.
Arguments:
- lin_query: bfloat16 [2048, 4096], P('seq', 'head'), may hold values from -2 to 2
- lin_key: bfloat16 [2048, 4096], P('seq', 'head'), may hold values from -2 to 2
- lin_value: bfloat16 [2048, 4096], P('seq', 'head'), may hold values from -130 to 130
- log_decay: float32 [2048, 32], P('seq', 'head'), may hold values from -2 to 0
- gate_logits: bfloat16 [2048, 4096], P('seq', 'head'), may hold values from -6 to 6
- norm_gain: float32 [4096], P('head'), may hold values from 0.25 to 1.75
- soft_query: bfloat16 [2048, 4096], P('seq', 'head'), may hold values from -4 to 4
- soft_key: bfloat16 [2048, 4096], P('seq', 'head'), may hold values from -4 to 4
- soft_value: bfloat16 [2048, 4096], P('seq', 'head'), may hold values from -6 to 6
- doc_ids: int32 [2048], P('seq'), may hold values from 0 to 8, as said below
- doc_spans: int32 [9, 2], replicated, may hold values from 0 to 2048, as said below
Outputs:
- lin_out: bfloat16 [2048, 4096], P('seq', 'head')
- soft_out: bfloat16 [2048, 4096], P('seq', 'head')
The draws below stay inside these ranges and needn't reach their ends.
Inputs may be any that keep to these rules, and one draw needn't show every extreme that they name: `doc_ids`: never falls; document d covers exactly the positions doc_spans[d, 0] to doc_spans[d, 1] - 1. `doc_spans`: row 0 starts at 0, each row ends where the next starts, the last ends at 2048; every document holds 1 to 768 positions, and one holds exactly that many.
All inputs are finite; a program needn't handle non-finite values.
Results may differ from the reference program's by a relative error of at most 0.0053.
Values may be sent and summed in bfloat16 or wider, within the bound.
No kernel may reach another device: no remote copies, remote signals or barrier semaphores. Data moves between devices by JAX's collectives and lax.ppermute only.
A program may use at most 128 MiB of HBM per device.

```python
import jax
import jax.numpy as jnp
from jax import lax

HALF_MODEL_HEADS = 32
HD = 128
TOKENS_PER_SHARD = 256
SPAN = 3
CONTEXT_TOKENS = 2048


def layout(key):
    folded = jax.random.fold_in(key, 11)
    random_subkeys = jax.random.split(folded, 5)
    groups = CONTEXT_TOKENS // ((SPAN + 1) * TOKENS_PER_SHARD)
    longest = SPAN * TOKENS_PER_SHARD
    offset = TOKENS_PER_SHARD // 2
    middle = groups // 2
    group_index = jnp.arange(groups)
    totals = jnp.where(group_index == groups - 1, (SPAN + 1) * TOKENS_PER_SHARD - offset, (SPAN + 1) * TOKENS_PER_SHARD)
    leading = jax.random.randint(random_subkeys[0], (groups,), TOKENS_PER_SHARD, longest + 1)
    fixed_long = (group_index == middle) | (group_index == middle - 1)
    leading = jnp.where(fixed_long, longest, leading)
    remain = totals - leading
    second_len = jax.random.randint(random_subkeys[2], (groups,), 1, remain - 1)
    third_len = jax.random.randint(random_subkeys[3], (groups,), 1, remain - second_len)
    fourth_len = remain - second_len - third_len
    quads = jnp.stack([leading, second_len, third_len, fourth_len], axis=1)
    rotation = jax.random.randint(random_subkeys[4], (groups,), 0, 4)
    rotation = jnp.where(group_index == middle - 1, 1, jnp.where(group_index == middle, 0, rotation))
    order_table = (jnp.arange(4)[None, :] + rotation[:, None]) % 4
    body_lengths = jnp.take_along_axis(quads, order_table, axis=1).reshape(-1)
    lengths = jnp.concatenate([jnp.full((1,), offset, jnp.int32), body_lengths.astype(jnp.int32)]).astype(jnp.int32)
    ends = jnp.cumsum(lengths).astype(jnp.int32)
    starts = ends - lengths
    return (starts, ends)


def draw_doc_spans(key, part):
    starts, ends = layout(key)
    return jnp.stack([starts, ends], axis=1).astype(jnp.int32)


def draw_doc_ids(key, part):
    starts, ends = layout(key)
    positions = jnp.arange(CONTEXT_TOKENS, dtype=jnp.int32)
    counted = jnp.sum((positions[:, None] >= starts[None, :]).astype(jnp.int32), axis=1)
    return (counted - 1).astype(jnp.int32)


def draw_log_decay(key, part):
    random_subkeys = jax.random.split(key, 5)
    chain = SPAN * TOKENS_PER_SHARD
    lowest = 0.3 / chain
    highest = max(0.025, 3.0 / TOKENS_PER_SHARD)
    random_noise = 1.5 ** jax.random.uniform(random_subkeys[2], (CONTEXT_TOKENS, HALF_MODEL_HEADS), minval=-1.0, maxval=1.0)
    unit = jax.random.uniform(random_subkeys[0], (HALF_MODEL_HEADS,))
    decay_rates = lowest * (highest / lowest) ** unit
    devices = CONTEXT_TOKENS // TOKENS_PER_SHARD
    local = jax.random.uniform(random_subkeys[1], (devices, HALF_MODEL_HEADS), minval=-1.0, maxval=1.0)
    multiplier = jnp.repeat(2.0 ** local, TOKENS_PER_SHARD, axis=0)
    spike_amount = jax.random.randint(random_subkeys[3], (CONTEXT_TOKENS, HALF_MODEL_HEADS), 0, 2 * TOKENS_PER_SHARD) == 0
    loss_values = jax.random.uniform(random_subkeys[4], (CONTEXT_TOKENS, HALF_MODEL_HEADS), minval=0.2, maxval=0.5)
    return (-decay_rates[None, :] * multiplier * random_noise + jnp.where(spike_amount, jnp.log(1.0 - loss_values), 0.0)).astype(jnp.float32)


def draw_lin_value(key, part):
    random_subkeys = jax.random.split(key, 3)
    ramp = jnp.arange(HALF_MODEL_HEADS, dtype=jnp.float32) / (HALF_MODEL_HEADS - 1)
    entries = jnp.clip(jax.random.normal(random_subkeys[0], (CONTEXT_TOKENS, HALF_MODEL_HEADS * HD)), -4.0, 4.0)
    exponent = 0.5 * ramp + 0.5 * jax.random.uniform(random_subkeys[1], (HALF_MODEL_HEADS,))
    head_scale = jnp.repeat(10.0 ** exponent, HD)
    row_scale = 10.0 ** (0.5 * jax.random.uniform(random_subkeys[2], (CONTEXT_TOKENS, 1)))
    return (entries * head_scale[None, :] * row_scale).astype(jnp.bfloat16)


def query_key_pair(key):
    folded = jax.random.fold_in(key, 23)
    random_subkeys = jax.random.split(folded, 2)
    queries = jnp.clip(jax.random.normal(random_subkeys[0], (CONTEXT_TOKENS, HALF_MODEL_HEADS * HD)), -4.0, 4.0)
    keyed = jnp.clip(jax.random.normal(random_subkeys[1], (CONTEXT_TOKENS, HALF_MODEL_HEADS * HD)), -4.0, 4.0)
    return (queries.astype(jnp.float32), keyed.astype(jnp.float32))


def draw_soft_query(key, part):
    return query_key_pair(key)[0].astype(jnp.bfloat16)


def draw_soft_key(key, part):
    return query_key_pair(key)[1].astype(jnp.bfloat16)


def shard_levels(stream_key, extent, shards, smallest, largest):
    def one(dim, blocks):
        steps = jax.random.uniform(jax.random.fold_in(jax.random.fold_in(stream_key, 6), dim), (blocks,), jnp.float32, smallest / len(shards), largest / len(shards))
        return jnp.repeat(jnp.exp(steps), extent[dim] // blocks).reshape((-1,) + (1,) * (len(extent) - dim - 1))

    factor_of = one(*shards[0])
    for cut in shards[1:]:
        factor_of = factor_of * one(*cut)
    return factor_of


def bell_draw(rng, shape, deviation, most, pieces=(), kind=jnp.bfloat16):
    values = deviation * jax.random.normal(rng, shape, jnp.float32)
    if pieces:
        values = values * shard_levels(rng, shape, pieces, -0.22, 0.18)
    return jnp.clip(values, -most, most).astype(kind)


def setup_inputs(seed: int = 0) -> dict:
    seeds = jax.random.split(jax.random.key(seed), 12)
    lin_query = bell_draw(seeds[0], (CONTEXT_TOKENS, HALF_MODEL_HEADS * HD), 0.3, 2.0, ((0, 8), (1, 4)))
    lin_key = bell_draw(seeds[1], (CONTEXT_TOKENS, HALF_MODEL_HEADS * HD), 0.3, 2.0, ((0, 8), (1, 4)))
    lin_value = draw_lin_value(jax.random.fold_in(seeds[11], 71), 0)
    log_decay = draw_log_decay(jax.random.fold_in(seeds[11], 71), 0)
    gate_logits = bell_draw(seeds[4], (CONTEXT_TOKENS, HALF_MODEL_HEADS * HD), 1.0, 6.0, ((0, 8), (1, 4)))
    norm_gain = jnp.clip(1.0 + 0.15 * jax.random.normal(seeds[5], (HALF_MODEL_HEADS * HD,), jnp.float32), 0.25, 1.75)
    soft_query = draw_soft_query(jax.random.fold_in(seeds[11], 71), 0)
    soft_key = draw_soft_key(jax.random.fold_in(seeds[11], 71), 0)
    soft_value = bell_draw(seeds[8], (CONTEXT_TOKENS, HALF_MODEL_HEADS * HD), 1.0, 6.0, ((0, 8), (1, 4)))
    doc_ids = draw_doc_ids(jax.random.fold_in(seeds[11], 71), 0)
    doc_spans = draw_doc_spans(jax.random.fold_in(seeds[11], 71), 0)
    return {"lin_query": lin_query, "lin_key": lin_key, "lin_value": lin_value, "log_decay": log_decay, "gate_logits": gate_logits, "norm_gain": norm_gain, "soft_query": soft_query, "soft_key": soft_key, "soft_value": soft_value, "doc_ids": doc_ids, "doc_spans": doc_spans}


def halved(values):
    return lax.optimization_barrier(values.astype(jnp.bfloat16)).astype(jnp.float32)

def reference(lin_query, lin_key, lin_value, log_decay, gate_logits, norm_gain, soft_query, soft_key, soft_value, doc_ids, doc_spans):
    starts = doc_spans[:, 0][doc_ids].astype(jnp.int32)
    block_count = CONTEXT_TOKENS // TOKENS_PER_SHARD
    block_bases = jnp.arange(block_count, dtype=jnp.int32) * TOKENS_PER_SHARD

    def light_step(carried, item):
        query_block, key_block, value_block, decay_block, start_block, gate_block, block_base = item
        positions = block_base + jnp.arange(TOKENS_PER_SHARD, dtype=jnp.int32)
        cumulative = jnp.cumsum(decay_block, axis=0)
        scores = jnp.einsum('thd,shd->hts', query_block.astype(jnp.float32), key_block.astype(jnp.float32))
        spread = cumulative.T[:, :, None] - cumulative.T[:, None, :]
        allowed = (positions[None, :] <= positions[:, None]) & (positions[None, :] >= start_block[:, None])
        weights = jnp.where(allowed[None], scores * jnp.exp(jnp.minimum(spread, 0.0)), 0.0)
        inner_part = jnp.einsum('hts,shd->thd', halved(weights), value_block.astype(jnp.float32))
        last_cumul = cumulative[-1]
        tail_weight = jnp.where((positions >= start_block[-1])[:, None], jnp.exp(jnp.minimum(last_cumul[None, :] - cumulative, 0.0)), 0.0)
        tail_key = halved(key_block.astype(jnp.float32) * tail_weight[:, :, None])
        local_state = jnp.einsum('shd,she->hde', tail_key, value_block.astype(jnp.float32))
        local_decay = jnp.where(start_block[-1] < block_base, jnp.exp(last_cumul), 0.0)
        entry_scale = jnp.where((start_block < block_base)[:, None], jnp.exp(cumulative), 0.0)
        cross_part = jnp.einsum('thd,hde->the', query_block.astype(jnp.float32), halved(carried)) * entry_scale[:, :, None]
        mixture = inner_part + cross_part
        squares = lax.optimization_barrier(jnp.sum(mixture * mixture, axis=(1, 2)))
        norm_scale = lax.rsqrt(squares / (HALF_MODEL_HEADS * HD) + 1e-06)
        output = mixture.reshape(TOKENS_PER_SHARD, HALF_MODEL_HEADS * HD) * norm_scale[:, None] * norm_gain[None, :] * jax.nn.sigmoid(gate_block.astype(jnp.float32))
        renewed = local_decay[:, None, None] * carried + local_state
        return (renewed, output.astype(jnp.bfloat16))
    items = (lin_query.reshape(block_count, TOKENS_PER_SHARD, HALF_MODEL_HEADS, HD), lin_key.reshape(block_count, TOKENS_PER_SHARD, HALF_MODEL_HEADS, HD), lin_value.reshape(block_count, TOKENS_PER_SHARD, HALF_MODEL_HEADS, HD), log_decay.reshape(block_count, TOKENS_PER_SHARD, HALF_MODEL_HEADS), starts.reshape(block_count, TOKENS_PER_SHARD), gate_logits.reshape(block_count, TOKENS_PER_SHARD, HALF_MODEL_HEADS * HD), block_bases)
    _, lin_blocks = lax.scan(light_step, jnp.zeros((HALF_MODEL_HEADS, HD, HD), jnp.float32), items)
    lin_out = lin_blocks.reshape(CONTEXT_TOKENS, HALF_MODEL_HEADS * HD)
    margin = SPAN * TOKENS_PER_SHARD
    padded_keys = jnp.pad(soft_key.reshape(CONTEXT_TOKENS, HALF_MODEL_HEADS, HD), ((margin, 0), (0, 0), (0, 0)))
    padded_values = jnp.pad(soft_value.reshape(CONTEXT_TOKENS, HALF_MODEL_HEADS, HD), ((margin, 0), (0, 0), (0, 0)))

    def soft_block(item):
        query_block, start_block, block_base = item
        key_block = lax.dynamic_slice_in_dim(padded_keys, block_base.astype(jnp.int32), margin + TOKENS_PER_SHARD, 0)
        value_block = lax.dynamic_slice_in_dim(padded_values, block_base.astype(jnp.int32), margin + TOKENS_PER_SHARD, 0)
        positions = block_base + jnp.arange(TOKENS_PER_SHARD, dtype=jnp.int32)
        key_pos = block_base - margin + jnp.arange(margin + TOKENS_PER_SHARD, dtype=jnp.int32)
        visible = (key_pos[None, :] >= start_block[:, None]) & (key_pos[None, :] <= positions[:, None])
        logits = jnp.einsum('thd,shd->hts', query_block.astype(jnp.float32), key_block.astype(jnp.float32)) * HD ** (-0.5)
        logits = jnp.where(visible[None], logits, -jnp.inf)
        row_max = lax.optimization_barrier(jnp.max(logits, axis=2, keepdims=True))
        soft_weights = jnp.exp(logits - row_max)
        soft_total = lax.optimization_barrier(jnp.sum(soft_weights, axis=2))
        attended = jnp.einsum('hts,shd->thd', halved(soft_weights), value_block.astype(jnp.float32))
        return (attended / soft_total.T[:, :, None]).reshape(TOKENS_PER_SHARD, HALF_MODEL_HEADS * HD).astype(jnp.bfloat16)
    soft_blocks = lax.map(soft_block, (soft_query.reshape(block_count, TOKENS_PER_SHARD, HALF_MODEL_HEADS, HD), starts.reshape(block_count, TOKENS_PER_SHARD), block_bases))
    soft_out = soft_blocks.reshape(CONTEXT_TOKENS, HALF_MODEL_HEADS * HD)
    return (lin_out, soft_out)
```

```python
import functools

import jax
import jax.numpy as jnp
from jax import lax
from jax.experimental import pallas as pl
from jax.experimental.pallas import tpu as pltpu
from jax.sharding import PartitionSpec as P

HALF_MODEL_HEADS = 32
HD = 128
NEG = -1e30
SOFT_SCALE = HD ** (-0.5) * 1.4426950408889634
F32 = jnp.float32
BF16 = jnp.bfloat16
VMEM_LIMIT = 48 * 1024 * 1024


def dot(a, b, dims, precision=None):
    return lax.dot_general(a, b, (dims, ((), ())), precision=precision, preferred_element_type=F32)


def row_starts(spans_ref, rows, base):
    positions = base + lax.broadcasted_iota(jnp.int32, (rows, 1), 0)

    def one(d, starts):
        first = spans_ref[d, 0]
        return jnp.where(positions >= first, jnp.maximum(starts, first), starts)

    docs = spans_ref.shape[0]
    return lax.fori_loop(0, docs, one, jnp.zeros((rows, 1), jnp.int32), unroll=docs <= 16), positions


def last_start(spans_ref, last):
    def one(d, start):
        first = spans_ref[d, 0]
        return jnp.where(first <= last, jnp.maximum(start, first), start)

    docs = spans_ref.shape[0]
    return lax.fori_loop(0, docs, one, jnp.int32(0), unroll=docs <= 16)


def split3(x):
    high = x.astype(BF16)
    rest = x - high.astype(F32)
    middle = rest.astype(BF16)
    return high, middle, (rest - middle.astype(F32)).astype(BF16)


def running_sums(decay):
    rows = decay.shape[0]
    r = lax.broadcasted_iota(jnp.int32, (rows, rows), 0)
    c = lax.broadcasted_iota(jnp.int32, (rows, rows), 1)
    lower = jnp.where(c <= r, 1.0, 0.0).astype(BF16)
    column = sum(dot(lower, part, ((1,), (0,))) for part in split3(decay))
    return column


def state_kernel(spans_ref, decay_ref, k_ref, v_ref, pack_ref, state_ref, cum_ref, dec_ref):
    rows, width = k_ref.shape
    heads = width // HD
    base = lax.axis_index("seq") * rows
    cumulative = running_sums(decay_ref[...])
    cum_ref[...] = cumulative
    start = last_start(spans_ref, base + rows - 1)
    positions = base + lax.broadcasted_iota(jnp.int32, (rows, 1), 0)
    inside = positions >= start
    last = cumulative[rows - 1 : rows, :]
    tail = jnp.where(inside, jnp.exp(jnp.minimum(last - cumulative, 0.0)), 0.0)
    block_decay = jnp.where(start < base, jnp.exp(last), 0.0)
    low_rows = []
    high_rows = []
    for h in range(heads):
        cols = slice(h * HD, (h + 1) * HD)
        tail_key = (k_ref[:, cols].astype(F32) * tail[:, h : h + 1]).astype(BF16)
        state = dot(tail_key, v_ref[:, cols], ((0,), (0,)))
        state_ref[cols, :] = state
        pack_ref[cols, :] = state.astype(BF16)
        one = jnp.broadcast_to(block_decay[:, h : h + 1], (1, HD))
        dec_ref[h : h + 1, :] = one
        high = one.astype(BF16)
        high_rows.append(high.astype(F32))
        low_rows.append(one - high.astype(F32))
    pad = [jnp.zeros((1, HD), F32)] * (pack_ref.shape[0] - width - 2 * heads)
    pack_ref[width:, :] = jnp.concatenate(high_rows + low_rows + pad, axis=0).astype(BF16)


def pair_kernel(state_ref, dec_ref, from_ref, out_ref):
    width = state_ref.shape[0]
    for h in range(width // HD):
        cols = slice(h * HD, (h + 1) * HD)
        out_ref[cols, :] = (
            state_ref[cols, :] + dec_ref[h : h + 1, :] * from_ref[cols, :].astype(F32)
        ).astype(BF16)


def lin_kernel(
    spans_ref, q_ref, k_ref, v_ref, gate_ref, gain_ref, cum_ref, one_ref, two_ref, y_ref, sq_ref
):
    rows, width = k_ref.shape
    heads = width // HD
    base = lax.axis_index("seq") * rows
    starts, positions = row_starts(spans_ref, rows, base)
    cumulative = cum_ref[...]
    across = jnp.transpose(cumulative)
    s_pos = base + lax.broadcasted_iota(jnp.int32, (rows, rows), 1)
    allowed = (s_pos <= positions) & (s_pos >= starts)
    entry = jnp.where(starts < base, jnp.exp(cumulative), 0.0)
    mix_gain = gain_ref[...]
    squares = jnp.zeros((rows, 1), F32)
    extra = one_ref[width:, :].astype(F32)
    for h in range(heads):
        cols = slice(h * HD, (h + 1) * HD)
        q = q_ref[:, cols]
        v = v_ref[:, cols]
        scores = dot(q, k_ref[:, cols], ((1,), (1,)))
        spread = cumulative[:, h : h + 1] - across[h : h + 1, :]
        weights = jnp.where(allowed, scores * jnp.exp(jnp.minimum(spread, 0.0)), 0.0).astype(BF16)
        before = extra[h : h + 1, :] + extra[heads + h : heads + h + 1, :]
        carried = one_ref[cols, :].astype(F32) + before * two_ref[cols, :].astype(F32)
        mixture = dot(weights, v, ((1,), (0,))) + (
            dot(q, carried.astype(BF16), ((1,), (0,))) * entry[:, h : h + 1]
        )
        squares = squares + jnp.sum(mixture * mixture, axis=1, keepdims=True)
        gate = jax.nn.sigmoid(gate_ref[:, cols].astype(F32))
        y_ref[:, cols] = mixture * mix_gain[:, cols] * gate
    sq_ref[...] = jnp.transpose(jnp.broadcast_to(squares, (rows, HD)))[:8, :]


def visible(starts, base_of_keys, rows):
    keys = base_of_keys + lax.broadcasted_iota(jnp.int32, (rows, rows), 1)
    return keys, keys >= starts


def soft_first_kernel(
    spans_ref, q_ref, k0_ref, v0_ref, k2_ref, v2_ref, ke_ref, ve_ref, acc_ref, m_ref, l_ref
):
    rows, width = q_ref.shape
    heads = width // HD
    place = lax.axis_index("seq")
    base = place * rows
    odd = lax.rem(place, 2)
    starts, positions = row_starts(spans_ref, rows, base)
    keys, seen = visible(starts, base, rows)
    bias0 = jnp.where(seen & (keys <= positions), 0.0, NEG)
    bias2 = jnp.where(visible(starts, base - 2 * rows, rows)[1], 0.0, NEG)
    biase = jnp.where(visible(starts, base - (1 + 2 * odd) * rows, rows)[1], 0.0, NEG)
    for h in range(heads):
        cols = slice(h * HD, (h + 1) * HD)
        q = q_ref[:, cols]
        s0 = dot(q, k0_ref[:, cols], ((1,), (1,))) * SOFT_SCALE + bias0
        s2 = dot(q, k2_ref[:, cols], ((1,), (1,))) * SOFT_SCALE + bias2
        se = dot(q, ke_ref[:, cols], ((1,), (1,))) * SOFT_SCALE + biase
        m = jnp.max(jnp.maximum(jnp.maximum(s0, s2), se), axis=1, keepdims=True)
        p0 = jnp.exp2(s0 - m)
        p2 = jnp.exp2(s2 - m)
        pe = jnp.exp2(se - m)
        m_ref[:, h : h + 1] = m
        l_ref[:, h : h + 1] = jnp.sum(p0 + p2 + pe, axis=1, keepdims=True)
        acc_ref[:, cols] = (
            dot(p0.astype(BF16), v0_ref[:, cols], ((1,), (0,)))
            + dot(p2.astype(BF16), v2_ref[:, cols], ((1,), (0,)))
            + dot(pe.astype(BF16), ve_ref[:, cols], ((1,), (0,)))
        )


def soft_last_kernel(
    spans_ref, q_ref, kx_ref, vx_ref, kf_ref, vf_ref, acc_ref, m_ref, l_ref, y_ref, total_ref,
    soft_ref, lin_ref,
):
    rows, width = q_ref.shape
    heads = width // HD
    place = lax.axis_index("seq")
    base = place * rows
    odd = lax.rem(place, 2)
    starts, _ = row_starts(spans_ref, rows, base)
    bias = jnp.where(visible(starts, base - (3 - 2 * odd) * rows, rows)[1], 0.0, NEG)
    total = jnp.transpose(total_ref[...])[:, 0:1]
    norm = lax.rsqrt(total / (HALF_MODEL_HEADS * HD) + 1e-06)
    m_all = m_ref[...]
    l_all = l_ref[...]
    pick = odd == 1
    for h in range(heads):
        cols = slice(h * HD, (h + 1) * HD)
        q = q_ref[:, cols]
        k = jnp.where(pick, kx_ref[:, cols], kf_ref[:, cols])
        v = jnp.where(pick, vx_ref[:, cols], vf_ref[:, cols])
        s = dot(q, k, ((1,), (1,))) * SOFT_SCALE + bias
        m_old = m_all[:, h : h + 1]
        m = jnp.maximum(m_old, jnp.max(s, axis=1, keepdims=True))
        p = jnp.exp2(s - m)
        shrink = jnp.exp2(m_old - m)
        weight = l_all[:, h : h + 1] * shrink + jnp.sum(p, axis=1, keepdims=True)
        acc = acc_ref[:, cols] * shrink + dot(p.astype(BF16), v, ((1,), (0,)))
        soft_ref[:, cols] = (acc / weight).astype(BF16)
        lin_ref[:, cols] = (y_ref[:, cols] * norm).astype(BF16)


SMEM = pl.BlockSpec(memory_space=pltpu.SMEM)
FULL = pl.BlockSpec(memory_space=pltpu.VMEM)


def call(kernel, name, out_shape, arrays, smem=1):
    return pl.pallas_call(
        kernel,
        name=name,
        out_shape=out_shape,
        in_specs=[SMEM] * smem + [FULL] * (len(arrays) - smem),
        out_specs=jax.tree.map(lambda _: FULL, out_shape),
        compiler_params=pltpu.CompilerParams(vmem_limit_bytes=VMEM_LIMIT),
    )(*arrays)


def shards(
    lin_query,
    lin_key,
    lin_value,
    log_decay,
    gate_logits,
    norm_gain,
    soft_query,
    soft_key,
    soft_value,
    doc_ids,
    doc_spans,
):
    rows, width = lin_query.shape
    heads = width // HD
    devices = lax.axis_size("seq")
    shape = jax.ShapeDtypeStruct

    def ahead(array, by, step=1):
        return lax.ppermute(
            array, "seq", [(i, i + by) for i in range(0, devices - by, step)]
        )

    def swap(array):
        return lax.ppermute(array, "seq", [(i, i ^ 1) for i in range(devices)])

    k2 = ahead(soft_key, 2)
    kx = ahead(soft_key, 1, 2)
    v2 = ahead(soft_value, 2)
    vx = ahead(soft_value, 1, 2)
    ke = swap(k2)
    ve = swap(v2)
    kf = ahead(ke, 2, 2)
    vf = ahead(ve, 2, 2)

    extra = -(-2 * heads // 16) * 16
    pack, state, cumulative, decay = call(
        state_kernel,
        "state",
        (
            shape((width + extra, HD), BF16),
            shape((width, HD), F32),
            shape((rows, heads), F32),
            shape((heads, HD), F32),
        ),
        (doc_spans, log_decay, lin_key, lin_value),
    )
    one = ahead(pack, 1)
    pair = call(pair_kernel, "pair", shape((width, HD), BF16), (state, decay, one), smem=0)
    two = ahead(pair, 2)
    y, squares = call(
        lin_kernel,
        "lin",
        (shape((rows, width), F32), shape((8, rows), F32)),
        (
            doc_spans, lin_query, lin_key, lin_value, gate_logits, norm_gain.reshape(1, width),
            cumulative, one, two,
        ),
    )
    total = lax.psum(squares, "head")
    acc, top, weight = call(
        soft_first_kernel,
        "soft_first",
        (shape((rows, width), F32), shape((rows, heads), F32), shape((rows, heads), F32)),
        (doc_spans, soft_query, soft_key, soft_value, k2, v2, ke, ve),
    )
    soft_out, lin_out = call(
        soft_last_kernel,
        "soft_last",
        (shape((rows, width), BF16), shape((rows, width), BF16)),
        (doc_spans, soft_query, kx, vx, kf, vf, acc, top, weight, y, total),
    )
    return (lin_out, soft_out)


def solution(mesh):
    in_specs = (
        P("seq", "head"),
        P("seq", "head"),
        P("seq", "head"),
        P("seq", "head"),
        P("seq", "head"),
        P("head"),
        P("seq", "head"),
        P("seq", "head"),
        P("seq", "head"),
        P("seq"),
        P(),
    )
    out_specs = (P("seq", "head"), P("seq", "head"))
    return jax.shard_map(shards, mesh=mesh, in_specs=in_specs, out_specs=out_specs, check_vma=False)
```

```python
import functools

import jax
import jax.numpy as jnp
from jax import lax
from jax.experimental import pallas as pl
from jax.experimental.pallas import tpu as pltpu
from jax.sharding import PartitionSpec as P

HALF_MODEL_HEADS = 32
HD = 128
LANES = 128
NEG = -1e30
SOFT_SCALE = HD ** (-0.5) * 1.4426950408889634
F32 = jnp.float32
BF16 = jnp.bfloat16
VMEM_LIMIT = 6 * 1024 * 1024


def dot(a, b, dims):
    return lax.dot_general(a, b, (dims, ((), ())), preferred_element_type=F32)


def wide(column, width):
    return jnp.concatenate([column] * (width // LANES), axis=1)


def split3(x):
    high = x.astype(BF16)
    rest = x - high.astype(F32)
    middle = rest.astype(BF16)
    return high, middle, (rest - middle.astype(F32)).astype(BF16)


def places(rows):
    base = lax.axis_index("seq") * rows
    return base, base + lax.broadcasted_iota(jnp.int32, (rows, LANES), 0)


def prep_kernel(spans_ref, decay_ref, starts_ref, last_ref, cum_ref, across_ref):
    rows, width = cum_ref.shape
    heads = width // HD
    base, positions = places(rows)
    last_position = jnp.zeros((8, LANES), jnp.int32) + (base + rows - 1)

    def one(d, starts):
        first = spans_ref[0, d]
        return tuple(
            jnp.where(at >= first, jnp.maximum(start, first), start)
            for start, at in zip(starts, (positions, last_position))
        )

    docs = spans_ref.shape[1]
    nothing = (jnp.zeros_like(positions), jnp.zeros_like(last_position))
    starts_ref[...], last_ref[...] = lax.fori_loop(0, docs, one, nothing, unroll=docs <= 16)
    r = lax.broadcasted_iota(jnp.int32, (rows, rows), 0)
    c = lax.broadcasted_iota(jnp.int32, (rows, rows), 1)
    upper = jnp.where(r <= c, 1.0, 0.0).astype(BF16)
    across = sum(dot(part, upper, ((1,), (0,))) for part in split3(decay_ref[...]))
    across_ref[...] = across
    head = lax.broadcasted_iota(jnp.int32, (heads, width), 0)
    lane = lax.broadcasted_iota(jnp.int32, (heads, width), 1)
    spread = jnp.where((lane >= head * HD) & (lane < (head + 1) * HD), 1.0, 0.0).astype(BF16)
    cum_ref[...] = sum(dot(part, spread, ((0,), (0,))) for part in split3(across))


def key_bias(starts_ref, rows, keys, behind):
    base, positions = places(rows)
    key = base - behind + lax.broadcasted_iota(jnp.int32, (rows, keys), 1)
    seen = (key >= wide(starts_ref[...], keys)) & (key <= wide(positions, keys))
    return jnp.where(seen, 0.0, NEG)


def state_kernel(last_ref, cum_ref, k_ref, v_ref, pack_ref, state_ref, dec_ref):
    rows, width = k_ref.shape
    base, positions = places(rows)
    start = last_ref[0:1, :]
    inside = positions >= start
    for h in range(width // HD):
        cols = slice(h * HD, (h + 1) * HD)
        mine = cum_ref[:, cols]
        last = mine[rows - 1 : rows, :]
        tail = jnp.where(inside, jnp.exp(jnp.minimum(last - mine, 0.0)), 0.0)
        tail_key = (k_ref[:, cols].astype(F32) * tail).astype(BF16)
        state = dot(tail_key, v_ref[:, cols], ((0,), (0,)))
        state_ref[:, cols] = state
        pack_ref[0:HD, cols] = state.astype(BF16)
        decay = jnp.broadcast_to(jnp.where(start < base, jnp.exp(last), 0.0), (8, HD))
        dec_ref[:, cols] = decay
        high = decay.astype(BF16).astype(F32)
        pack_ref[HD:, cols] = jnp.concatenate([high, decay - high], axis=0).astype(BF16)


def pick_kernel(there_ref, own_ref, out_ref):
    odd = lax.rem(lax.axis_index("seq"), 2) == 1

    @pl.when(odd)
    def _():
        out_ref[...] = there_ref[...]

    @pl.when(jnp.logical_not(odd))
    def _():
        out_ref[...] = own_ref[...]


def pair_kernel(state_ref, dec_ref, from_ref, k_ref, out_ref):
    reach = out_ref.shape[0] - HD
    out_ref[0:HD, :] = (
        state_ref[...] + dec_ref[0:1, :] * from_ref[0:HD, :].astype(F32)
    ).astype(BF16)
    out_ref[HD:, :] = k_ref[k_ref.shape[0] - reach :, :]


def nearest_kernel(v_ref, out_ref):
    out_ref[...] = v_ref[v_ref.shape[0] - out_ref.shape[0] :, :]


def lin_kernel(
    starts_ref, q_ref, k_ref, v_ref, gate_ref, gain_ref, cum_ref, across_ref, one_ref, two_ref,
    y_ref, sq_ref,
):
    rows, width = k_ref.shape
    heads = width // HD
    allowed = key_bias(starts_ref, rows, rows, 0) == 0.0
    base, _ = places(rows)
    enters = starts_ref[...] < base
    squares = jnp.zeros((rows, HD), F32)
    extra = one_ref[HD:, :].astype(F32)
    for h in range(heads):
        cols = slice(h * HD, (h + 1) * HD)
        before = extra[0:1, cols] + extra[8:9, cols]
        carried = one_ref[0:HD, cols].astype(F32) + before * two_ref[0:HD, cols].astype(F32)
        mine = cum_ref[:, cols]
        decayed = jnp.exp(jnp.minimum(wide(mine, rows) - across_ref[h : h + 1, :], 0.0))
        q = q_ref[:, cols]
        scores = dot(q, k_ref[:, cols], ((1,), (1,)))
        weights = jnp.where(allowed, scores * decayed, 0.0).astype(BF16)
        cross = dot(q, carried.astype(BF16), ((1,), (0,)))
        mixture = dot(weights, v_ref[:, cols], ((1,), (0,))) + (
            cross * jnp.where(enters, jnp.exp(mine), 0.0)
        )
        squares = squares + mixture * mixture
        gate = jax.nn.sigmoid(gate_ref[:, cols].astype(F32))
        y_ref[:, cols] = mixture * gain_ref[:, cols] * gate
    ones = jnp.ones((8, HD), BF16)
    sq_ref[...] = sum(dot(ones, part, ((1,), (1,))) for part in split3(squares))


def norm_kernel(y_ref, *refs):
    *parts, lin_ref = refs
    total = jnp.transpose(sum(part[...] for part in parts))[:, 0:1]
    norm = lax.rsqrt(total / (HALF_MODEL_HEADS * HD) + 1e-06)
    lin_ref[...] = (y_ref[...] * norm).astype(BF16)


def with_ones(v):
    return jnp.concatenate([v, jnp.ones_like(v)], axis=1)


def top_of(s):
    return jnp.broadcast_to(jnp.max(s, axis=1, keepdims=True), (s.shape[0], LANES))


def soft_own_kernel(starts_ref, q_ref, k_ref, v_ref, sums_ref, m_ref):
    rows, width = q_ref.shape
    bias = key_bias(starts_ref, rows, rows, 0)
    for h in range(width // HD):
        cols = slice(h * HD, (h + 1) * HD)
        s = dot(q_ref[:, cols], k_ref[:, cols], ((1,), (1,))) * SOFT_SCALE + bias
        m = top_of(s)
        m_ref[:, cols] = m
        p = jnp.exp2(s - wide(m, rows)).astype(BF16)
        sums_ref[:, 2 * h * HD : 2 * (h + 1) * HD] = dot(p, with_ones(v_ref[:, cols]), ((1,), (0,)))


def soft_grow_kernel(back, starts_ref, q_ref, k_ref, v_ref, sums0_ref, m0_ref, sums_ref, m_ref):
    rows, width = q_ref.shape
    keys = k_ref.shape[0]
    bias = key_bias(starts_ref, rows, keys, back * rows)
    for h in range(width // HD):
        cols = slice(h * HD, (h + 1) * HD)
        both = slice(2 * h * HD, 2 * (h + 1) * HD)
        m_old = m0_ref[:, cols]
        s = dot(q_ref[:, cols], k_ref[:, cols], ((1,), (1,))) * SOFT_SCALE + bias
        m = jnp.maximum(m_old, top_of(s))
        m_ref[:, cols] = m
        p = jnp.exp2(s - wide(m, keys)).astype(BF16)
        sums_ref[:, both] = sums0_ref[:, both] * wide(jnp.exp2(m_old - m), 2 * HD) + dot(
            p, with_ones(v_ref[:, cols]), ((1,), (0,))
        )


def soft_weigh_kernel(back, starts_ref, q_ref, k_ref, sums_ref, m_ref, p_ref, acc_ref, inv_ref):
    rows, width = q_ref.shape
    keys = k_ref.shape[0] - HD
    bias = key_bias(starts_ref, rows, keys, (back - 1) * rows + keys)
    ones = jnp.ones((keys, HD), BF16)
    for h in range(width // HD):
        cols = slice(h * HD, (h + 1) * HD)
        m_old = m_ref[:, cols]
        s = dot(q_ref[:, cols], k_ref[HD:, cols], ((1,), (1,))) * SOFT_SCALE + bias
        m = jnp.maximum(m_old, top_of(s))
        p = jnp.exp2(s - wide(m, keys)).astype(BF16)
        shrink = jnp.exp2(m_old - m)
        weight = sums_ref[:, (2 * h + 1) * HD : (2 * h + 2) * HD] * shrink + dot(
            p, ones, ((1,), (0,))
        )
        inv = 1.0 / weight
        p_ref[:, h * keys : (h + 1) * keys] = p
        acc_ref[:, cols] = sums_ref[:, 2 * h * HD : (2 * h + 1) * HD] * (shrink * inv)
        inv_ref[:, cols] = inv


def soft_last_kernel(p_ref, v_ref, acc_ref, inv_ref, soft_ref):
    keys = v_ref.shape[0]
    for h in range(acc_ref.shape[1] // HD):
        cols = slice(h * HD, (h + 1) * HD)
        more = dot(p_ref[:, h * keys : (h + 1) * keys], v_ref[:, cols], ((1,), (0,)))
        soft_ref[:, cols] = (acc_ref[:, cols] + more * inv_ref[:, cols]).astype(BF16)


SMEM = pl.BlockSpec(memory_space=pltpu.SMEM)
VMEM = pl.BlockSpec(memory_space=pltpu.VMEM)


def call(kernel, name, out_shape, *arrays, smem=0):
    return pl.pallas_call(
        kernel,
        name=name,
        out_shape=out_shape,
        in_specs=[SMEM] * smem + [VMEM] * (len(arrays) - smem),
        out_specs=jax.tree.map(lambda _: VMEM, out_shape),
        compiler_params=pltpu.CompilerParams(vmem_limit_bytes=VMEM_LIMIT),
    )(*arrays)


def program(
    reach,
    lin_query,
    lin_key,
    lin_value,
    log_decay,
    gate_logits,
    norm_gain,
    soft_query,
    soft_key,
    soft_value,
    doc_spans,
):
    rows, width = lin_query.shape
    heads = width // HD
    devices = lax.axis_size("seq")
    shape = jax.ShapeDtypeStruct

    def ahead(array, by):
        return lax.ppermute(array, "seq", [(i, i + by) for i in range(devices - by)])

    def swap(array):
        return lax.ppermute(array, "seq", [(i, i ^ 1) for i in range(devices)])

    def everywhere(array):
        count = lax.axis_size("head")
        return [array] + [
            lax.ppermute(array, "head", [(i, (i + by) % count) for i in range(count)])
            for by in range(1, count)
        ]

    together = lax.optimization_barrier
    sums = (shape((rows, 2 * width), F32), shape((rows, width), F32))
    half = shape((rows, width), BF16)

    starts, last_start, cumulative, across = call(
        prep_kernel,
        "prep",
        (
            shape((rows, LANES), jnp.int32),
            shape((8, LANES), jnp.int32),
            shape((rows, width), F32),
            shape((heads, rows), F32),
        ),
        doc_spans.T, log_decay.T, smem=1,
    )
    first_key, starts = together((soft_key, starts))
    k2 = ahead(first_key, 2)
    pack, state, decay = call(
        state_kernel,
        "state",
        (shape((HD + 16, width), BF16), shape((HD, width), F32), shape((8, width), F32)),
        last_start, cumulative, lin_key, lin_value,
    )
    own_value, pack = together((soft_value, pack))
    one = ahead(pack, 1)
    v2 = ahead(own_value, 2)
    soft = call(soft_own_kernel, "soft_own", sums, starts, soft_query, soft_key, soft_value)
    own_key, top = together((soft_key, soft[1]))
    soft = (soft[0], top)
    k1 = swap(call(pick_kernel, "pick_k", half, k2, own_key))
    v1 = swap(call(pick_kernel, "pick_v", half, v2, soft_value))
    pair = call(
        pair_kernel, "pair", shape((HD + reach, width), BF16), state, decay, one, k1
    )
    two = ahead(pair, 2)
    soft = call(
        functools.partial(soft_grow_kernel, 2), "soft_2", sums, starts, soft_query, k2, v2, *soft
    )
    v1, top = together((v1, soft[1]))
    soft = (soft[0], top)
    v3 = ahead(call(nearest_kernel, "nearest", shape((reach, width), BF16), v1), 2)
    y, squares = call(
        lin_kernel,
        "lin",
        (shape((rows, width), F32), shape((8, rows), F32)),
        starts, lin_query, lin_key, lin_value, gate_logits, norm_gain.reshape(1, width),
        cumulative, across, one, two,
    )
    parts = everywhere(squares)
    soft = call(
        functools.partial(soft_grow_kernel, 1), "soft_1", sums, starts, soft_query, k1, v1, *soft
    )
    lin_out = call(norm_kernel, "norm", half, y, *parts)
    weights, acc, inv = call(
        functools.partial(soft_weigh_kernel, 3), "soft_weigh",
        (
            shape((rows, heads * reach), BF16), shape((rows, width), F32),
            shape((rows, width), F32),
        ),
        starts, soft_query, two, *soft,
    )
    soft_out = call(soft_last_kernel, "soft_last", half, weights, v3, acc, inv)
    return (lin_out, soft_out)


def shards(
    lin_query,
    lin_key,
    lin_value,
    log_decay,
    gate_logits,
    norm_gain,
    soft_query,
    soft_key,
    soft_value,
    doc_ids,
    doc_spans,
):
    rows = lin_query.shape[0]
    blocks = rows * jnp.arange(lax.axis_size("seq"), dtype=jnp.int32)
    begun = doc_spans[None, :, 0] <= blocks[:, None]
    starts = jnp.max(jnp.where(begun, doc_spans[None, :, 0], 0), axis=1)
    farthest = jnp.max(blocks - starts)
    reach = rows // 2
    return lax.cond(
        farthest <= 2 * rows + reach,
        functools.partial(program, reach),
        functools.partial(program, rows),
        lin_query, lin_key, lin_value, log_decay, gate_logits, norm_gain, soft_query, soft_key,
        soft_value, doc_spans,
    )


def solution(mesh):
    in_specs = (
        P("seq", "head"),
        P("seq", "head"),
        P("seq", "head"),
        P("seq", "head"),
        P("seq", "head"),
        P("head"),
        P("seq", "head"),
        P("seq", "head"),
        P("seq", "head"),
        P("seq"),
        P(),
    )
    out_specs = (P("seq", "head"), P("seq", "head"))
    return jax.shard_map(shards, mesh=mesh, in_specs=in_specs, out_specs=out_specs, check_vma=False)
```

```python
import functools

import jax
import jax.numpy as jnp
from jax import lax
from jax.experimental import pallas as pl
from jax.experimental.pallas import tpu as pltpu
from jax.sharding import PartitionSpec as P

HALF_MODEL_HEADS = 32
HD = 128
LANES = 128
NEG = -1e30
SOFT_SCALE = HD ** (-0.5) * 1.4426950408889634
F32 = jnp.float32
BF16 = jnp.bfloat16
VMEM_LIMIT = 6 * 1024 * 1024


def dot(a, b, dims):
    return lax.dot_general(a, b, (dims, ((), ())), preferred_element_type=F32)


def wide(column, width):
    return jnp.concatenate([column] * (width // LANES), axis=1)


def split3(x):
    high = x.astype(BF16)
    rest = x - high.astype(F32)
    middle = rest.astype(BF16)
    return high, middle, (rest - middle.astype(F32)).astype(BF16)


def places(rows):
    base = lax.axis_index("seq") * rows
    return base, base + lax.broadcasted_iota(jnp.int32, (rows, LANES), 0)


def prep_kernel(spans_ref, decay_ref, starts_ref, last_ref, cum_ref, across_ref):
    rows, width = cum_ref.shape
    heads = width // HD
    base, positions = places(rows)
    last_position = jnp.zeros((8, LANES), jnp.int32) + (base + rows - 1)

    def one(d, starts):
        first = spans_ref[0, d]
        return tuple(
            jnp.where(at >= first, jnp.maximum(start, first), start)
            for start, at in zip(starts, (positions, last_position))
        )

    docs = spans_ref.shape[1]
    nothing = (jnp.zeros_like(positions), jnp.zeros_like(last_position))
    starts_ref[...], last_ref[...] = lax.fori_loop(0, docs, one, nothing, unroll=docs <= 16)
    r = lax.broadcasted_iota(jnp.int32, (rows, rows), 0)
    c = lax.broadcasted_iota(jnp.int32, (rows, rows), 1)
    upper = jnp.where(r <= c, 1.0, 0.0).astype(BF16)
    across = sum(dot(part, upper, ((1,), (0,))) for part in split3(decay_ref[...]))
    across_ref[...] = across
    head = lax.broadcasted_iota(jnp.int32, (heads, width), 0)
    lane = lax.broadcasted_iota(jnp.int32, (heads, width), 1)
    spread = jnp.where((lane >= head * HD) & (lane < (head + 1) * HD), 1.0, 0.0).astype(BF16)
    cum_ref[...] = sum(dot(part, spread, ((0,), (0,))) for part in split3(across))


def key_bias(starts_ref, rows, keys, behind):
    base, positions = places(rows)
    key = base - behind + lax.broadcasted_iota(jnp.int32, (rows, keys), 1)
    seen = (key >= wide(starts_ref[...], keys)) & (key <= wide(positions, keys))
    return jnp.where(seen, 0.0, NEG)


def state_kernel(last_ref, cum_ref, k_ref, v_ref, pack_ref, state_ref, dec_ref):
    rows, width = k_ref.shape
    base, positions = places(rows)
    start = last_ref[0:1, :]
    inside = positions >= start
    for h in range(width // HD):
        cols = slice(h * HD, (h + 1) * HD)
        mine = cum_ref[:, cols]
        last = mine[rows - 1 : rows, :]
        tail = jnp.where(inside, jnp.exp(jnp.minimum(last - mine, 0.0)), 0.0)
        tail_key = (k_ref[:, cols].astype(F32) * tail).astype(BF16)
        state = dot(tail_key, v_ref[:, cols], ((0,), (0,)))
        state_ref[:, cols] = state
        pack_ref[0:HD, cols] = state.astype(BF16)
        decay = jnp.broadcast_to(jnp.where(start < base, jnp.exp(last), 0.0), (8, HD))
        dec_ref[:, cols] = decay
        high = decay.astype(BF16).astype(F32)
        pack_ref[HD:, cols] = jnp.concatenate([high, decay - high], axis=0).astype(BF16)


def pick_kernel(there_ref, own_ref, out_ref):
    odd = lax.rem(lax.axis_index("seq"), 2) == 1

    @pl.when(odd)
    def _():
        out_ref[...] = there_ref[...]

    @pl.when(jnp.logical_not(odd))
    def _():
        out_ref[...] = own_ref[...]


def decays_of(pack_ref):
    return pack_ref[HD : HD + 1, :].astype(F32) + pack_ref[HD + 8 : HD + 9, :].astype(F32)


def pair_kernel(state_ref, dec_ref, other_ref, far_ref, k_ref, out_ref):
    reach = out_ref.shape[0] - HD
    odd = lax.rem(lax.axis_index("seq"), 2) == 1
    other, other_decay = other_ref[0:HD, :].astype(F32), decays_of(other_ref)
    own, own_decay = state_ref[...], dec_ref[0:1, :]

    @pl.when(odd)
    def _():
        out_ref[0:HD, :] = (own + own_decay * other).astype(BF16)

    @pl.when(jnp.logical_not(odd))
    def _():
        first = own + own_decay * far_ref[0:HD, :].astype(F32)
        out_ref[0:HD, :] = (other + other_decay * first).astype(BF16)

    out_ref[HD:, :] = k_ref[k_ref.shape[0] - reach :, :]


def nearest_kernel(v_ref, out_ref):
    out_ref[...] = v_ref[v_ref.shape[0] - out_ref.shape[0] :, :]


def lin_kernel(
    starts_ref, q_ref, k_ref, v_ref, gate_ref, gain_ref, cum_ref, across_ref, other_ref, two_ref,
    y_ref, sq_ref,
):
    rows, width = k_ref.shape
    heads = width // HD
    allowed = key_bias(starts_ref, rows, rows, 0) == 0.0
    base, _ = places(rows)
    enters = starts_ref[...] < base
    squares = jnp.zeros((rows, HD), F32)
    odd = lax.rem(lax.axis_index("seq"), 2) == 1
    kept = jnp.where(odd, 1.0, 0.0)
    passed = jnp.where(odd, decays_of(other_ref), 1.0)
    for h in range(heads):
        cols = slice(h * HD, (h + 1) * HD)
        carried = (
            kept * other_ref[0:HD, cols].astype(F32)
            + passed[:, cols] * two_ref[0:HD, cols].astype(F32)
        )
        mine = cum_ref[:, cols]
        decayed = jnp.exp(jnp.minimum(wide(mine, rows) - across_ref[h : h + 1, :], 0.0))
        q = q_ref[:, cols]
        scores = dot(q, k_ref[:, cols], ((1,), (1,)))
        weights = jnp.where(allowed, scores * decayed, 0.0).astype(BF16)
        cross = dot(q, carried.astype(BF16), ((1,), (0,)))
        mixture = dot(weights, v_ref[:, cols], ((1,), (0,))) + (
            cross * jnp.where(enters, jnp.exp(mine), 0.0)
        )
        squares = squares + mixture * mixture
        gate = jax.nn.sigmoid(gate_ref[:, cols].astype(F32))
        y_ref[:, cols] = mixture * gain_ref[:, cols] * gate
    ones = jnp.ones((8, HD), BF16)
    sq_ref[...] = sum(dot(ones, part, ((1,), (1,))) for part in split3(squares))


def norm_kernel(y_ref, *refs):
    *parts, lin_ref = refs
    total = jnp.transpose(sum(part[...] for part in parts))[:, 0:1]
    norm = lax.rsqrt(total / (HALF_MODEL_HEADS * HD) + 1e-06)
    lin_ref[...] = (y_ref[...] * norm).astype(BF16)


def with_ones(v):
    return jnp.concatenate([v, jnp.ones_like(v)], axis=1)


def top_of(s):
    return jnp.broadcast_to(jnp.max(s, axis=1, keepdims=True), (s.shape[0], LANES))


def soft_own_kernel(starts_ref, q_ref, k_ref, v_ref, sums_ref, m_ref):
    rows, width = q_ref.shape
    bias = key_bias(starts_ref, rows, rows, 0)
    for h in range(width // HD):
        cols = slice(h * HD, (h + 1) * HD)
        s = dot(q_ref[:, cols], k_ref[:, cols], ((1,), (1,))) * SOFT_SCALE + bias
        m = top_of(s)
        m_ref[:, cols] = m
        p = jnp.exp2(s - wide(m, rows)).astype(BF16)
        sums_ref[:, 2 * h * HD : 2 * (h + 1) * HD] = dot(p, with_ones(v_ref[:, cols]), ((1,), (0,)))


def soft_grow_kernel(back, starts_ref, q_ref, k_ref, v_ref, sums0_ref, m0_ref, sums_ref, m_ref):
    rows, width = q_ref.shape
    keys = k_ref.shape[0]
    bias = key_bias(starts_ref, rows, keys, back * rows)
    for h in range(width // HD):
        cols = slice(h * HD, (h + 1) * HD)
        both = slice(2 * h * HD, 2 * (h + 1) * HD)
        m_old = m0_ref[:, cols]
        s = dot(q_ref[:, cols], k_ref[:, cols], ((1,), (1,))) * SOFT_SCALE + bias
        m = jnp.maximum(m_old, top_of(s))
        m_ref[:, cols] = m
        p = jnp.exp2(s - wide(m, keys)).astype(BF16)
        sums_ref[:, both] = sums0_ref[:, both] * wide(jnp.exp2(m_old - m), 2 * HD) + dot(
            p, with_ones(v_ref[:, cols]), ((1,), (0,))
        )


def soft_weigh_kernel(back, starts_ref, q_ref, k_ref, sums_ref, m_ref, p_ref, acc_ref, inv_ref):
    rows, width = q_ref.shape
    keys = k_ref.shape[0] - HD
    bias = key_bias(starts_ref, rows, keys, (back - 1) * rows + keys)
    ones = jnp.ones((keys, HD), BF16)
    for h in range(width // HD):
        cols = slice(h * HD, (h + 1) * HD)
        m_old = m_ref[:, cols]
        s = dot(q_ref[:, cols], k_ref[HD:, cols], ((1,), (1,))) * SOFT_SCALE + bias
        m = jnp.maximum(m_old, top_of(s))
        p = jnp.exp2(s - wide(m, keys)).astype(BF16)
        shrink = jnp.exp2(m_old - m)
        weight = sums_ref[:, (2 * h + 1) * HD : (2 * h + 2) * HD] * shrink + dot(
            p, ones, ((1,), (0,))
        )
        inv = 1.0 / weight
        p_ref[:, h * keys : (h + 1) * keys] = p
        acc_ref[:, cols] = sums_ref[:, 2 * h * HD : (2 * h + 1) * HD] * (shrink * inv)
        inv_ref[:, cols] = inv


def soft_last_kernel(p_ref, v_ref, acc_ref, inv_ref, soft_ref):
    keys = v_ref.shape[0]
    for h in range(acc_ref.shape[1] // HD):
        cols = slice(h * HD, (h + 1) * HD)
        more = dot(p_ref[:, h * keys : (h + 1) * keys], v_ref[:, cols], ((1,), (0,)))
        soft_ref[:, cols] = (acc_ref[:, cols] + more * inv_ref[:, cols]).astype(BF16)


SMEM = pl.BlockSpec(memory_space=pltpu.SMEM)
VMEM = pl.BlockSpec(memory_space=pltpu.VMEM)


def call(kernel, name, out_shape, *arrays, smem=0):
    return pl.pallas_call(
        kernel,
        name=name,
        out_shape=out_shape,
        in_specs=[SMEM] * smem + [VMEM] * (len(arrays) - smem),
        out_specs=jax.tree.map(lambda _: VMEM, out_shape),
        compiler_params=pltpu.CompilerParams(vmem_limit_bytes=VMEM_LIMIT),
    )(*arrays)


def program(
    reach,
    lin_query,
    lin_key,
    lin_value,
    log_decay,
    gate_logits,
    norm_gain,
    soft_query,
    soft_key,
    soft_value,
    doc_spans,
):
    rows, width = lin_query.shape
    heads = width // HD
    devices = lax.axis_size("seq")
    shape = jax.ShapeDtypeStruct

    def ahead(array, by, step=1):
        return lax.ppermute(
            array, "seq", [(i, i + by) for i in range(0, devices - by, step)]
        )

    def swap(array):
        return lax.ppermute(array, "seq", [(i, i ^ 1) for i in range(devices)])

    def everywhere(array):
        count = lax.axis_size("head")
        return [array] + [
            lax.ppermute(array, "head", [(i, (i + by) % count) for i in range(count)])
            for by in range(1, count)
        ]

    together = lax.optimization_barrier
    sums = (shape((rows, 2 * width), F32), shape((rows, width), F32))
    half = shape((rows, width), BF16)

    starts, last_start, cumulative, across = call(
        prep_kernel,
        "prep",
        (
            shape((rows, LANES), jnp.int32),
            shape((8, LANES), jnp.int32),
            shape((rows, width), F32),
            shape((heads, rows), F32),
        ),
        doc_spans.T, log_decay.T, smem=1,
    )
    k2 = ahead(soft_key, 2)
    pack, state, decay = call(
        state_kernel,
        "state",
        (shape((HD + 16, width), BF16), shape((HD, width), F32), shape((8, width), F32)),
        last_start, cumulative, lin_key, lin_value,
    )
    other = swap(pack)
    own_value, pack = together((soft_value, pack))
    v2 = ahead(own_value, 2)
    soft = call(soft_own_kernel, "soft_own", sums, starts, soft_query, soft_key, soft_value)
    own_key, top = together((soft_key, soft[1]))
    soft = (soft[0], top)
    k1 = swap(call(pick_kernel, "pick_k", half, k2, own_key))
    far = ahead(other, 2, 2)
    v1 = swap(call(pick_kernel, "pick_v", half, v2, soft_value))
    pair = call(
        pair_kernel, "pair", shape((HD + reach, width), BF16), state, decay, other, far, k1
    )
    two = ahead(pair, 2)
    soft = call(
        functools.partial(soft_grow_kernel, 2), "soft_2", sums, starts, soft_query, k2, v2, *soft
    )
    v1, top = together((v1, soft[1]))
    soft = (soft[0], top)
    v3 = ahead(call(nearest_kernel, "nearest", shape((reach, width), BF16), v1), 2)
    soft = call(
        functools.partial(soft_grow_kernel, 1), "soft_1", sums, starts, soft_query, k1, v1, *soft
    )
    two, top = together((two, soft[1]))
    soft = (soft[0], top)
    y, squares = call(
        lin_kernel,
        "lin",
        (shape((rows, width), F32), shape((8, rows), F32)),
        starts, lin_query, lin_key, lin_value, gate_logits, norm_gain.reshape(1, width),
        cumulative, across, other, two,
    )
    parts = everywhere(squares)
    lin_out = call(norm_kernel, "norm", half, y, *parts)
    weights, acc, inv = call(
        functools.partial(soft_weigh_kernel, 3), "soft_weigh",
        (
            shape((rows, heads * reach), BF16), shape((rows, width), F32),
            shape((rows, width), F32),
        ),
        starts, soft_query, two, *soft,
    )
    soft_out = call(soft_last_kernel, "soft_last", half, weights, v3, acc, inv)
    return (lin_out, soft_out)


def shards(
    lin_query,
    lin_key,
    lin_value,
    log_decay,
    gate_logits,
    norm_gain,
    soft_query,
    soft_key,
    soft_value,
    doc_ids,
    doc_spans,
):
    rows = lin_query.shape[0]
    blocks = rows * jnp.arange(lax.axis_size("seq"), dtype=jnp.int32)
    begun = doc_spans[None, :, 0] <= blocks[:, None]
    starts = jnp.max(jnp.where(begun, doc_spans[None, :, 0], 0), axis=1)
    farthest = jnp.max(blocks - starts)
    reach = rows // 2
    return lax.cond(
        farthest <= 2 * rows + reach,
        functools.partial(program, reach),
        functools.partial(program, rows),
        lin_query, lin_key, lin_value, log_decay, gate_logits, norm_gain, soft_query, soft_key,
        soft_value, doc_spans,
    )


def solution(mesh):
    in_specs = (
        P("seq", "head"),
        P("seq", "head"),
        P("seq", "head"),
        P("seq", "head"),
        P("seq", "head"),
        P("head"),
        P("seq", "head"),
        P("seq", "head"),
        P("seq", "head"),
        P("seq"),
        P(),
    )
    out_specs = (P("seq", "head"), P("seq", "head"))
    return jax.shard_map(shards, mesh=mesh, in_specs=in_specs, out_specs=out_specs, check_vma=False)
```

```python
import functools

import jax
import jax.numpy as jnp
from jax import lax
from jax.experimental import pallas as pl
from jax.experimental.pallas import tpu as pltpu
from jax.sharding import PartitionSpec as P

HALF_MODEL_HEADS = 32
HD = 128
SPAN = 3
LANES = 128
NEG = -1e30
SOFT_SCALE = HD ** (-0.5) * 1.4426950408889634
F32 = jnp.float32
BF16 = jnp.bfloat16
VMEM_LIMIT = 6 * 1024 * 1024


def dot(a, b, dims):
    return lax.dot_general(a, b, (dims, ((), ())), preferred_element_type=F32)


def wide(column, width):
    return jnp.concatenate([column] * (width // LANES), axis=1)


def split3(x):
    high = x.astype(BF16)
    rest = x - high.astype(F32)
    middle = rest.astype(BF16)
    return high, middle, (rest - middle.astype(F32)).astype(BF16)


def places(rows):
    base = lax.axis_index("seq") * rows
    return base, base + lax.broadcasted_iota(jnp.int32, (rows, LANES), 0)


def prep_kernel(spans_ref, decay_ref, starts_ref, last_ref, cum_ref, across_ref):
    rows, width = cum_ref.shape
    heads = width // HD
    base, positions = places(rows)
    last_position = jnp.zeros((8, LANES), jnp.int32) + (base + rows - 1)

    def one(d, starts):
        first = spans_ref[0, d]
        return tuple(
            jnp.where(at >= first, jnp.maximum(start, first), start)
            for start, at in zip(starts, (positions, last_position))
        )

    docs = spans_ref.shape[1]
    nothing = (jnp.zeros_like(positions), jnp.zeros_like(last_position))
    starts_ref[...], last_ref[...] = lax.fori_loop(0, docs, one, nothing, unroll=docs <= 16)
    r = lax.broadcasted_iota(jnp.int32, (rows, rows), 0)
    c = lax.broadcasted_iota(jnp.int32, (rows, rows), 1)
    upper = jnp.where(r <= c, 1.0, 0.0).astype(BF16)
    across = sum(dot(part, upper, ((1,), (0,))) for part in split3(decay_ref[...]))
    across_ref[...] = across
    head = lax.broadcasted_iota(jnp.int32, (heads, width), 0)
    lane = lax.broadcasted_iota(jnp.int32, (heads, width), 1)
    spread = jnp.where((lane >= head * HD) & (lane < (head + 1) * HD), 1.0, 0.0).astype(BF16)
    cum_ref[...] = sum(dot(part, spread, ((0,), (0,))) for part in split3(across))


def key_bias(starts_ref, rows, keys, behind):
    base, positions = places(rows)
    key = base - behind + lax.broadcasted_iota(jnp.int32, (rows, keys), 1)
    seen = (key >= wide(starts_ref[...], keys)) & (key <= wide(positions, keys))
    return jnp.where(seen, 0.0, NEG)


def state_kernel(last_ref, cum_ref, k_ref, v_ref, pack_ref, state_ref, dec_ref):
    rows, width = k_ref.shape
    base, positions = places(rows)
    start = last_ref[0:1, :]
    inside = positions >= start
    for h in range(width // HD):
        cols = slice(h * HD, (h + 1) * HD)
        mine = cum_ref[:, cols]
        last = mine[rows - 1 : rows, :]
        tail = jnp.where(inside, jnp.exp(jnp.minimum(last - mine, 0.0)), 0.0)
        tail_key = (k_ref[:, cols].astype(F32) * tail).astype(BF16)
        state = dot(tail_key, v_ref[:, cols], ((0,), (0,)))
        state_ref[:, cols] = state
        pack_ref[0:HD, cols] = state.astype(BF16)
        decay = jnp.broadcast_to(jnp.where(start < base, jnp.exp(last), 0.0), (8, HD))
        dec_ref[:, cols] = decay
        high = decay.astype(BF16).astype(F32)
        pack_ref[HD:, cols] = jnp.concatenate([high, decay - high], axis=0).astype(BF16)


def pick_kernel(there_ref, own_ref, out_ref):
    odd = lax.rem(lax.axis_index("seq"), 2) == 1

    @pl.when(odd)
    def _():
        out_ref[...] = there_ref[...]

    @pl.when(jnp.logical_not(odd))
    def _():
        out_ref[...] = own_ref[...]


def decays_of(pack_ref):
    return pack_ref[HD : HD + 1, :].astype(F32) + pack_ref[HD + 8 : HD + 9, :].astype(F32)


def pair_kernel(state_ref, dec_ref, other_ref, far_ref, k_ref, out_ref):
    reach = out_ref.shape[0] - HD
    odd = lax.rem(lax.axis_index("seq"), 2) == 1
    other, other_decay = other_ref[0:HD, :].astype(F32), decays_of(other_ref)
    own, own_decay = state_ref[...], dec_ref[0:1, :]

    @pl.when(odd)
    def _():
        out_ref[0:HD, :] = (own + own_decay * other).astype(BF16)

    @pl.when(jnp.logical_not(odd))
    def _():
        first = own + own_decay * far_ref[0:HD, :].astype(F32)
        out_ref[0:HD, :] = (other + other_decay * first).astype(BF16)

    out_ref[HD:, :] = k_ref[k_ref.shape[0] - reach :, :]


def nearest_kernel(v_ref, out_ref):
    out_ref[...] = v_ref[v_ref.shape[0] - out_ref.shape[0] :, :]


def inner_kernel(
    starts_ref, q_ref, k_ref, v_ref, gate_ref, gain_ref, cum_ref, across_ref, inner_ref, scale_ref
):
    rows, width = k_ref.shape
    allowed = key_bias(starts_ref, rows, rows, 0) == 0.0
    for h in range(width // HD):
        cols = slice(h * HD, (h + 1) * HD)
        decayed = jnp.exp(jnp.minimum(wide(cum_ref[:, cols], rows) - across_ref[h : h + 1, :], 0.0))
        scores = dot(q_ref[:, cols], k_ref[:, cols], ((1,), (1,)))
        weights = jnp.where(allowed, scores * decayed, 0.0).astype(BF16)
        inner_ref[:, cols] = dot(weights, v_ref[:, cols], ((1,), (0,)))
        scale_ref[:, cols] = gain_ref[:, cols] * jax.nn.sigmoid(gate_ref[:, cols].astype(F32))


def cross_kernel(
    starts_ref, q_ref, cum_ref, inner_ref, other_ref, two_ref, mixture_ref, sq_ref
):
    rows, width = q_ref.shape
    base, _ = places(rows)
    enters = starts_ref[...] < base
    odd = lax.rem(lax.axis_index("seq"), 2) == 1
    kept = jnp.where(odd, 1.0, 0.0)
    passed = jnp.where(odd, decays_of(other_ref), 1.0)
    squares = jnp.zeros((rows, HD), F32)
    for h in range(width // HD):
        cols = slice(h * HD, (h + 1) * HD)
        carried = (
            kept * other_ref[0:HD, cols].astype(F32)
            + passed[:, cols] * two_ref[0:HD, cols].astype(F32)
        )
        cross = dot(q_ref[:, cols], carried.astype(BF16), ((1,), (0,)))
        mixture = inner_ref[:, cols] + cross * jnp.where(enters, jnp.exp(cum_ref[:, cols]), 0.0)
        squares = squares + mixture * mixture
        mixture_ref[:, cols] = mixture
    ones = jnp.ones((8, HD), BF16)
    sq_ref[...] = sum(dot(ones, part, ((1,), (1,))) for part in split3(squares))


def with_ones(v):
    return jnp.concatenate([v, jnp.ones_like(v)], axis=1)


def top_of(s):
    return jnp.broadcast_to(jnp.max(s, axis=1, keepdims=True), (s.shape[0], LANES))


def soft_own_kernel(starts_ref, q_ref, k_ref, v_ref, sums_ref, m_ref):
    rows, width = q_ref.shape
    bias = key_bias(starts_ref, rows, rows, 0)
    for h in range(width // HD):
        cols = slice(h * HD, (h + 1) * HD)
        s = dot(q_ref[:, cols], k_ref[:, cols], ((1,), (1,))) * SOFT_SCALE + bias
        m = top_of(s)
        m_ref[:, cols] = m
        p = jnp.exp2(s - wide(m, rows)).astype(BF16)
        sums_ref[:, 2 * h * HD : 2 * (h + 1) * HD] = dot(p, with_ones(v_ref[:, cols]), ((1,), (0,)))


def soft_grow_kernel(back, starts_ref, q_ref, k_ref, v_ref, sums0_ref, m0_ref, sums_ref, m_ref):
    rows, width = q_ref.shape
    keys = k_ref.shape[0]
    bias = key_bias(starts_ref, rows, keys, back * rows)
    for h in range(width // HD):
        cols = slice(h * HD, (h + 1) * HD)
        both = slice(2 * h * HD, 2 * (h + 1) * HD)
        m_old = m0_ref[:, cols]
        s = dot(q_ref[:, cols], k_ref[:, cols], ((1,), (1,))) * SOFT_SCALE + bias
        m = jnp.maximum(m_old, top_of(s))
        m_ref[:, cols] = m
        p = jnp.exp2(s - wide(m, keys)).astype(BF16)
        sums_ref[:, both] = sums0_ref[:, both] * wide(jnp.exp2(m_old - m), 2 * HD) + dot(
            p, with_ones(v_ref[:, cols]), ((1,), (0,))
        )


def soft_weigh_kernel(back, starts_ref, q_ref, k_ref, sums_ref, m_ref, p_ref, acc_ref, inv_ref):
    rows, width = q_ref.shape
    keys = k_ref.shape[0] - HD
    bias = key_bias(starts_ref, rows, keys, (back - 1) * rows + keys)
    ones = jnp.ones((keys, HD), BF16)
    for h in range(width // HD):
        cols = slice(h * HD, (h + 1) * HD)
        m_old = m_ref[:, cols]
        s = dot(q_ref[:, cols], k_ref[HD:, cols], ((1,), (1,))) * SOFT_SCALE + bias
        m = jnp.maximum(m_old, top_of(s))
        p = jnp.exp2(s - wide(m, keys)).astype(BF16)
        shrink = jnp.exp2(m_old - m)
        weight = sums_ref[:, (2 * h + 1) * HD : (2 * h + 2) * HD] * shrink + dot(
            p, ones, ((1,), (0,))
        )
        inv = 1.0 / weight
        p_ref[:, h * keys : (h + 1) * keys] = p
        acc_ref[:, cols] = sums_ref[:, 2 * h * HD : (2 * h + 1) * HD] * (shrink * inv)
        inv_ref[:, cols] = inv


def last_kernel(p_ref, v_ref, acc_ref, inv_ref, mixture_ref, scale_ref, *refs):
    *parts, lin_ref, soft_ref = refs
    keys = v_ref.shape[0]
    total = jnp.transpose(sum(part[...] for part in parts))[:, 0:1]
    norm = jnp.broadcast_to(
        lax.rsqrt(total / (HALF_MODEL_HEADS * HD) + 1e-06), (acc_ref.shape[0], HD)
    )
    for h in range(acc_ref.shape[1] // HD):
        cols = slice(h * HD, (h + 1) * HD)
        more = dot(p_ref[:, h * keys : (h + 1) * keys], v_ref[:, cols], ((1,), (0,)))
        soft_ref[:, cols] = (acc_ref[:, cols] + more * inv_ref[:, cols]).astype(BF16)
        lin_ref[:, cols] = (mixture_ref[:, cols] * norm * scale_ref[:, cols]).astype(BF16)


SMEM = pl.BlockSpec(memory_space=pltpu.SMEM)
VMEM = pl.BlockSpec(memory_space=pltpu.VMEM)


def call(kernel, name, out_shape, *arrays, smem=0):
    return pl.pallas_call(
        kernel,
        name=name,
        out_shape=out_shape,
        in_specs=[SMEM] * smem + [VMEM] * (len(arrays) - smem),
        out_specs=jax.tree.map(lambda _: VMEM, out_shape),
        compiler_params=pltpu.CompilerParams(vmem_limit_bytes=VMEM_LIMIT),
    )(*arrays)


def program(
    reach,
    lin_query,
    lin_key,
    lin_value,
    log_decay,
    gate_logits,
    norm_gain,
    soft_query,
    soft_key,
    soft_value,
    doc_spans,
):
    rows, width = lin_query.shape
    heads = width // HD
    devices = lax.axis_size("seq")
    shape = jax.ShapeDtypeStruct

    def ahead(array, by, step=1):
        return lax.ppermute(
            array, "seq", [(i, i + by) for i in range(0, devices - by, step)]
        )

    def swap(array):
        return lax.ppermute(array, "seq", [(i, i ^ 1) for i in range(devices)])

    def everywhere(array):
        count = lax.axis_size("head")
        return [array] + [
            lax.ppermute(array, "head", [(i, (i + by) % count) for i in range(count)])
            for by in range(1, count)
        ]

    together = lax.optimization_barrier
    sums = (shape((rows, 2 * width), F32), shape((rows, width), F32))
    half = shape((rows, width), BF16)

    starts, last_start, cumulative, across = call(
        prep_kernel,
        "prep",
        (
            shape((rows, LANES), jnp.int32),
            shape((8, LANES), jnp.int32),
            shape((rows, width), F32),
            shape((heads, rows), F32),
        ),
        doc_spans.T, log_decay.T, smem=1,
    )
    k2 = ahead(soft_key, 2)
    pack, state, decay = call(
        state_kernel,
        "state",
        (shape((HD + 16, width), BF16), shape((HD, width), F32), shape((8, width), F32)),
        last_start, cumulative, lin_key, lin_value,
    )
    other = swap(pack)
    own_value, pack = together((soft_value, pack))
    v2 = ahead(own_value, 2)
    soft = call(soft_own_kernel, "soft_own", sums, starts, soft_query, soft_key, soft_value)
    own_key, top = together((soft_key, soft[1]))
    soft = (soft[0], top)
    k1 = swap(call(pick_kernel, "pick_k", half, k2, own_key))
    far = ahead(other, 2, 2)
    v1 = swap(call(pick_kernel, "pick_v", half, v2, soft_value))
    pair = call(
        pair_kernel, "pair", shape((HD + reach, width), BF16), state, decay, other, far, k1
    )
    two = ahead(pair, 2)
    soft = call(
        functools.partial(soft_grow_kernel, 2), "soft_2", sums, starts, soft_query, k2, v2, *soft
    )
    inner, scale = call(
        inner_kernel, "inner", (shape((rows, width), F32), shape((rows, width), F32)),
        starts, lin_query, lin_key, lin_value, gate_logits, norm_gain.reshape(1, width),
        cumulative, across,
    )
    v1, top, inner = together((v1, soft[1], inner))
    soft = (soft[0], top)
    v3 = ahead(call(nearest_kernel, "nearest", shape((reach, width), BF16), v1), 2)
    soft = call(
        functools.partial(soft_grow_kernel, 1), "soft_1", sums, starts, soft_query, k1, v1, *soft
    )
    two, top = together((two, soft[1]))
    soft = (soft[0], top)
    mixture, squares = call(
        cross_kernel, "cross", (shape((rows, width), F32), shape((8, rows), F32)),
        starts, lin_query, cumulative, inner, other, two,
    )
    parts = everywhere(squares)
    weights, acc, inv = call(
        functools.partial(soft_weigh_kernel, SPAN), "soft_weigh",
        (
            shape((rows, heads * reach), BF16), shape((rows, width), F32),
            shape((rows, width), F32),
        ),
        starts, soft_query, two, *soft,
    )
    return call(
        last_kernel, "last", (half, half), weights, v3, acc, inv, mixture, scale, *parts
    )


def shards(
    lin_query,
    lin_key,
    lin_value,
    log_decay,
    gate_logits,
    norm_gain,
    soft_query,
    soft_key,
    soft_value,
    doc_ids,
    doc_spans,
):
    rows = lin_query.shape[0]
    reach = rows // 2
    firsts, ends = doc_spans[:, 0], doc_spans[:, 1]
    farthest = jnp.max((ends - 1) // rows * rows - firsts)
    return lax.cond(
        farthest <= (SPAN - 1) * rows + reach,
        functools.partial(program, reach),
        functools.partial(program, rows),
        lin_query, lin_key, lin_value, log_decay, gate_logits, norm_gain, soft_query, soft_key,
        soft_value, doc_spans,
    )


def solution(mesh):
    in_specs = (
        P("seq", "head"),
        P("seq", "head"),
        P("seq", "head"),
        P("seq", "head"),
        P("seq", "head"),
        P("head"),
        P("seq", "head"),
        P("seq", "head"),
        P("seq", "head"),
        P("seq"),
        P(),
    )
    out_specs = (P("seq", "head"), P("seq", "head"))
    return jax.shard_map(shards, mesh=mesh, in_specs=in_specs, out_specs=out_specs, check_vma=False)
```

```python
import functools

import jax
import jax.numpy as jnp
from jax import lax
from jax.experimental import pallas as pl
from jax.experimental.pallas import tpu as pltpu
from jax.sharding import PartitionSpec as P

HALF_MODEL_HEADS = 32
HD = 128
SPAN = 3
LANES = 128
NEG = -1e30
SOFT_SCALE = HD ** (-0.5) * 1.4426950408889634
F32 = jnp.float32
BF16 = jnp.bfloat16
VMEM_LIMIT = 6 * 1024 * 1024


def dot(a, b, dims):
    return lax.dot_general(a, b, (dims, ((), ())), preferred_element_type=F32)


def wide(column, width):
    return jnp.concatenate([column] * (width // LANES), axis=1)


def split3(x):
    high = x.astype(BF16)
    rest = x - high.astype(F32)
    middle = rest.astype(BF16)
    return high, middle, (rest - middle.astype(F32)).astype(BF16)


def places(rows):
    base = lax.axis_index("seq") * rows
    return base, base + lax.broadcasted_iota(jnp.int32, (rows, LANES), 0)


def prep_kernel(spans_ref, decay_ref, starts_ref, last_ref, cum_ref, across_ref):
    rows, width = cum_ref.shape
    heads = width // HD
    base, positions = places(rows)
    last_position = jnp.zeros((8, LANES), jnp.int32) + (base + rows - 1)

    def one(d, starts):
        first = spans_ref[0, d]
        return tuple(
            jnp.where(at >= first, jnp.maximum(start, first), start)
            for start, at in zip(starts, (positions, last_position))
        )

    docs = spans_ref.shape[1]
    nothing = (jnp.zeros_like(positions), jnp.zeros_like(last_position))
    starts_ref[...], last_ref[...] = lax.fori_loop(0, docs, one, nothing, unroll=docs <= 16)
    r = lax.broadcasted_iota(jnp.int32, (rows, rows), 0)
    c = lax.broadcasted_iota(jnp.int32, (rows, rows), 1)
    upper = jnp.where(r <= c, 1.0, 0.0).astype(BF16)
    across = sum(dot(part, upper, ((1,), (0,))) for part in split3(decay_ref[...]))
    across_ref[...] = across
    head = lax.broadcasted_iota(jnp.int32, (heads, width), 0)
    lane = lax.broadcasted_iota(jnp.int32, (heads, width), 1)
    spread = jnp.where((lane >= head * HD) & (lane < (head + 1) * HD), 1.0, 0.0).astype(BF16)
    cum_ref[...] = sum(dot(part, spread, ((0,), (0,))) for part in split3(across))


def key_bias(starts_ref, rows, keys, behind):
    base, positions = places(rows)
    key = base - behind + lax.broadcasted_iota(jnp.int32, (rows, keys), 1)
    seen = (key >= wide(starts_ref[...], keys)) & (key <= wide(positions, keys))
    return jnp.where(seen, 0.0, NEG)


def state_kernel(last_ref, cum_ref, k_ref, v_ref, pack_ref, state_ref, dec_ref):
    rows, width = k_ref.shape
    base, positions = places(rows)
    start = last_ref[0:1, :]
    inside = positions >= start
    for h in range(width // HD):
        cols = slice(h * HD, (h + 1) * HD)
        mine = cum_ref[:, cols]
        last = mine[rows - 1 : rows, :]
        tail = jnp.where(inside, jnp.exp(jnp.minimum(last - mine, 0.0)), 0.0)
        tail_key = (k_ref[:, cols].astype(F32) * tail).astype(BF16)
        state = dot(tail_key, v_ref[:, cols], ((0,), (0,)))
        state_ref[:, cols] = state
        pack_ref[0:HD, cols] = state.astype(BF16)
        decay = jnp.broadcast_to(jnp.where(start < base, jnp.exp(last), 0.0), (8, HD))
        dec_ref[:, cols] = decay
        high = decay.astype(BF16).astype(F32)
        pack_ref[HD:, cols] = jnp.concatenate([high, decay - high], axis=0).astype(BF16)


def pick_kernel(there_ref, own_ref, out_ref):
    odd = lax.rem(lax.axis_index("seq"), 2) == 1

    @pl.when(odd)
    def _():
        out_ref[...] = there_ref[...]

    @pl.when(jnp.logical_not(odd))
    def _():
        out_ref[...] = own_ref[...]


def decays_of(pack_ref):
    return pack_ref[HD : HD + 1, :].astype(F32) + pack_ref[HD + 8 : HD + 9, :].astype(F32)


def pair_kernel(state_ref, dec_ref, other_ref, far_ref, k_ref, out_ref):
    reach = out_ref.shape[0] - HD
    odd = lax.rem(lax.axis_index("seq"), 2) == 1
    other, other_decay = other_ref[0:HD, :].astype(F32), decays_of(other_ref)
    own, own_decay = state_ref[...], dec_ref[0:1, :]

    @pl.when(odd)
    def _():
        out_ref[0:HD, :] = (own + own_decay * other).astype(BF16)

    @pl.when(jnp.logical_not(odd))
    def _():
        first = own + own_decay * far_ref[...].astype(F32)
        out_ref[0:HD, :] = (other + other_decay * first).astype(BF16)

    out_ref[HD:, :] = k_ref[k_ref.shape[0] - reach :, :]


def first_kernel(a_ref, out_ref):
    out_ref[...] = a_ref[0 : out_ref.shape[0], :]


def nearest_kernel(v_ref, out_ref):
    out_ref[...] = v_ref[v_ref.shape[0] - out_ref.shape[0] :, :]


def inner_kernel(
    starts_ref, q_ref, k_ref, v_ref, gate_ref, gain_ref, cum_ref, across_ref, inner_ref, scale_ref
):
    rows, width = k_ref.shape
    allowed = key_bias(starts_ref, rows, rows, 0) == 0.0
    for h in range(width // HD):
        cols = slice(h * HD, (h + 1) * HD)
        decayed = jnp.exp(jnp.minimum(wide(cum_ref[:, cols], rows) - across_ref[h : h + 1, :], 0.0))
        scores = dot(q_ref[:, cols], k_ref[:, cols], ((1,), (1,)))
        weights = jnp.where(allowed, scores * decayed, 0.0).astype(BF16)
        inner_ref[:, cols] = dot(weights, v_ref[:, cols], ((1,), (0,)))
        scale_ref[:, cols] = gain_ref[:, cols] * jax.nn.sigmoid(gate_ref[:, cols].astype(F32))


def cross_kernel(
    starts_ref, q_ref, cum_ref, inner_ref, other_ref, two_ref, mixture_ref, sq_ref
):
    rows, width = q_ref.shape
    base, _ = places(rows)
    enters = starts_ref[...] < base
    odd = lax.rem(lax.axis_index("seq"), 2) == 1
    kept = jnp.where(odd, 1.0, 0.0)
    passed = jnp.where(odd, decays_of(other_ref), 1.0)
    squares = jnp.zeros((rows, HD), F32)
    for h in range(width // HD):
        cols = slice(h * HD, (h + 1) * HD)
        carried = (
            kept * other_ref[0:HD, cols].astype(F32)
            + passed[:, cols] * two_ref[0:HD, cols].astype(F32)
        )
        cross = dot(q_ref[:, cols], carried.astype(BF16), ((1,), (0,)))
        mixture = inner_ref[:, cols] + cross * jnp.where(enters, jnp.exp(cum_ref[:, cols]), 0.0)
        squares = squares + mixture * mixture
        mixture_ref[:, cols] = mixture
    ones = jnp.ones((8, HD), BF16)
    sq_ref[...] = sum(dot(ones, part, ((1,), (1,))) for part in split3(squares))


def with_ones(v):
    return jnp.concatenate([v, jnp.ones_like(v)], axis=1)


def top_of(s):
    return jnp.broadcast_to(jnp.max(s, axis=1, keepdims=True), (s.shape[0], LANES))


def soft_own_kernel(starts_ref, q_ref, k_ref, v_ref, sums_ref, m_ref):
    rows, width = q_ref.shape
    bias = key_bias(starts_ref, rows, rows, 0)
    for h in range(width // HD):
        cols = slice(h * HD, (h + 1) * HD)
        s = dot(q_ref[:, cols], k_ref[:, cols], ((1,), (1,))) * SOFT_SCALE + bias
        m = top_of(s)
        m_ref[:, cols] = m
        p = jnp.exp2(s - wide(m, rows)).astype(BF16)
        sums_ref[:, 2 * h * HD : 2 * (h + 1) * HD] = dot(p, with_ones(v_ref[:, cols]), ((1,), (0,)))


def soft_grow_kernel(back, starts_ref, q_ref, k_ref, v_ref, sums0_ref, m0_ref, sums_ref, m_ref):
    rows, width = q_ref.shape
    keys = k_ref.shape[0]
    bias = key_bias(starts_ref, rows, keys, back * rows)
    for h in range(width // HD):
        cols = slice(h * HD, (h + 1) * HD)
        both = slice(2 * h * HD, 2 * (h + 1) * HD)
        m_old = m0_ref[:, cols]
        s = dot(q_ref[:, cols], k_ref[:, cols], ((1,), (1,))) * SOFT_SCALE + bias
        m = jnp.maximum(m_old, top_of(s))
        m_ref[:, cols] = m
        p = jnp.exp2(s - wide(m, keys)).astype(BF16)
        sums_ref[:, both] = sums0_ref[:, both] * wide(jnp.exp2(m_old - m), 2 * HD) + dot(
            p, with_ones(v_ref[:, cols]), ((1,), (0,))
        )


def soft_weigh_kernel(back, starts_ref, q_ref, k_ref, sums_ref, m_ref, p_ref, acc_ref, inv_ref):
    rows, width = q_ref.shape
    keys = k_ref.shape[0] - HD
    bias = key_bias(starts_ref, rows, keys, (back - 1) * rows + keys)
    ones = jnp.ones((keys, HD), BF16)
    for h in range(width // HD):
        cols = slice(h * HD, (h + 1) * HD)
        m_old = m_ref[:, cols]
        s = dot(q_ref[:, cols], k_ref[HD:, cols], ((1,), (1,))) * SOFT_SCALE + bias
        m = jnp.maximum(m_old, top_of(s))
        p = jnp.exp2(s - wide(m, keys)).astype(BF16)
        shrink = jnp.exp2(m_old - m)
        weight = sums_ref[:, (2 * h + 1) * HD : (2 * h + 2) * HD] * shrink + dot(
            p, ones, ((1,), (0,))
        )
        inv = 1.0 / weight
        p_ref[:, h * keys : (h + 1) * keys] = p
        acc_ref[:, cols] = sums_ref[:, 2 * h * HD : (2 * h + 1) * HD] * (shrink * inv)
        inv_ref[:, cols] = inv


def last_kernel(p_ref, v_ref, acc_ref, inv_ref, mixture_ref, scale_ref, *refs):
    *parts, lin_ref, soft_ref = refs
    keys = v_ref.shape[0]
    total = jnp.transpose(sum(part[...] for part in parts))[:, 0:1]
    norm = jnp.broadcast_to(
        lax.rsqrt(total / (HALF_MODEL_HEADS * HD) + 1e-06), (acc_ref.shape[0], HD)
    )
    for h in range(acc_ref.shape[1] // HD):
        cols = slice(h * HD, (h + 1) * HD)
        more = dot(p_ref[:, h * keys : (h + 1) * keys], v_ref[:, cols], ((1,), (0,)))
        soft_ref[:, cols] = (acc_ref[:, cols] + more * inv_ref[:, cols]).astype(BF16)
        lin_ref[:, cols] = (mixture_ref[:, cols] * norm * scale_ref[:, cols]).astype(BF16)


SMEM = pl.BlockSpec(memory_space=pltpu.SMEM)
VMEM = pl.BlockSpec(memory_space=pltpu.VMEM)


def call(kernel, name, out_shape, *arrays, smem=0):
    return pl.pallas_call(
        kernel,
        name=name,
        out_shape=out_shape,
        in_specs=[SMEM] * smem + [VMEM] * (len(arrays) - smem),
        out_specs=jax.tree.map(lambda _: VMEM, out_shape),
        compiler_params=pltpu.CompilerParams(vmem_limit_bytes=VMEM_LIMIT),
    )(*arrays)


def program(
    reach,
    lin_query,
    lin_key,
    lin_value,
    log_decay,
    gate_logits,
    norm_gain,
    soft_query,
    soft_key,
    soft_value,
    doc_spans,
):
    rows, width = lin_query.shape
    heads = width // HD
    devices = lax.axis_size("seq")
    shape = jax.ShapeDtypeStruct

    def ahead(array, by, step=1):
        return lax.ppermute(
            array, "seq", [(i, i + by) for i in range(0, devices - by, step)]
        )

    def swap(array):
        return lax.ppermute(array, "seq", [(i, i ^ 1) for i in range(devices)])

    def everywhere(array):
        count = lax.axis_size("head")
        return [array] + [
            lax.ppermute(array, "head", [(i, (i + by) % count) for i in range(count)])
            for by in range(1, count)
        ]

    together = lax.optimization_barrier
    sums = (shape((rows, 2 * width), F32), shape((rows, width), F32))
    half = shape((rows, width), BF16)

    starts, last_start, cumulative, across = call(
        prep_kernel,
        "prep",
        (
            shape((rows, LANES), jnp.int32),
            shape((8, LANES), jnp.int32),
            shape((rows, width), F32),
            shape((heads, rows), F32),
        ),
        doc_spans.T, log_decay.T, smem=1,
    )
    k2 = ahead(soft_key, 2)
    pack, state, decay = call(
        state_kernel,
        "state",
        (shape((HD + 16, width), BF16), shape((HD, width), F32), shape((8, width), F32)),
        last_start, cumulative, lin_key, lin_value,
    )
    other = swap(pack)
    own_value, pack = together((soft_value, pack))
    v2 = ahead(own_value, 2)
    soft = call(soft_own_kernel, "soft_own", sums, starts, soft_query, soft_key, soft_value)
    own_key, top = together((soft_key, soft[1]))
    soft = (soft[0], top)
    k1 = swap(call(pick_kernel, "pick_k", half, k2, own_key))
    far = ahead(call(first_kernel, "states", shape((HD, width), BF16), other), 2, 2)
    v1 = swap(call(pick_kernel, "pick_v", half, v2, soft_value))
    pair = call(
        pair_kernel, "pair", shape((HD + reach, width), BF16), state, decay, other, far, k1
    )
    two = ahead(pair, 2)
    soft = call(
        functools.partial(soft_grow_kernel, 2), "soft_2", sums, starts, soft_query, k2, v2, *soft
    )
    inner, scale = call(
        inner_kernel, "inner", (shape((rows, width), F32), shape((rows, width), F32)),
        starts, lin_query, lin_key, lin_value, gate_logits, norm_gain.reshape(1, width),
        cumulative, across,
    )
    v1, top, inner = together((v1, soft[1], inner))
    soft = (soft[0], top)
    v3 = ahead(call(nearest_kernel, "nearest", shape((reach, width), BF16), v1), 2)
    soft = call(
        functools.partial(soft_grow_kernel, 1), "soft_1", sums, starts, soft_query, k1, v1, *soft
    )
    two, top = together((two, soft[1]))
    soft = (soft[0], top)
    mixture, squares = call(
        cross_kernel, "cross", (shape((rows, width), F32), shape((8, rows), F32)),
        starts, lin_query, cumulative, inner, other, two,
    )
    parts = everywhere(squares)
    weights, acc, inv = call(
        functools.partial(soft_weigh_kernel, SPAN), "soft_weigh",
        (
            shape((rows, heads * reach), BF16), shape((rows, width), F32),
            shape((rows, width), F32),
        ),
        starts, soft_query, two, *soft,
    )
    return call(
        last_kernel, "last", (half, half), weights, v3, acc, inv, mixture, scale, *parts
    )


def shards(
    lin_query,
    lin_key,
    lin_value,
    log_decay,
    gate_logits,
    norm_gain,
    soft_query,
    soft_key,
    soft_value,
    doc_ids,
    doc_spans,
):
    rows = lin_query.shape[0]
    reach = rows // 2
    firsts, lasts = doc_spans[:, 0], doc_spans[:, 1] - 1
    farthest = jnp.max(lasts - lax.rem(lasts, jnp.int32(rows)) - firsts)
    return lax.cond(
        farthest <= (SPAN - 1) * rows + reach,
        functools.partial(program, reach),
        functools.partial(program, rows),
        lin_query, lin_key, lin_value, log_decay, gate_logits, norm_gain, soft_query, soft_key,
        soft_value, doc_spans,
    )


def solution(mesh):
    in_specs = (
        P("seq", "head"),
        P("seq", "head"),
        P("seq", "head"),
        P("seq", "head"),
        P("seq", "head"),
        P("head"),
        P("seq", "head"),
        P("seq", "head"),
        P("seq", "head"),
        P("seq"),
        P(),
    )
    out_specs = (P("seq", "head"), P("seq", "head"))
    return jax.shard_map(shards, mesh=mesh, in_specs=in_specs, out_specs=out_specs, check_vma=False)
```

```python
import functools

import jax
import jax.numpy as jnp
from jax import lax
from jax.experimental import pallas as pl
from jax.experimental.pallas import tpu as pltpu
from jax.sharding import PartitionSpec as P

HALF_MODEL_HEADS = 32
HD = 128
SPAN = 3
LANES = 128
NEG = -1e30
SOFT_SCALE = HD ** (-0.5) * 1.4426950408889634
F32 = jnp.float32
BF16 = jnp.bfloat16
VMEM_LIMIT = 6 * 1024 * 1024


def dot(a, b, dims):
    return lax.dot_general(a, b, (dims, ((), ())), preferred_element_type=F32)


def wide(column, width):
    return jnp.concatenate([column] * (width // LANES), axis=1)


def split3(x):
    high = x.astype(BF16)
    rest = x - high.astype(F32)
    middle = rest.astype(BF16)
    return high, middle, (rest - middle.astype(F32)).astype(BF16)


def places(rows):
    base = lax.axis_index("seq") * rows
    return base, base + lax.broadcasted_iota(jnp.int32, (rows, LANES), 0)


def prep_kernel(spans_ref, decay_ref, starts_ref, last_ref, cum_ref, across_ref):
    rows, width = cum_ref.shape
    heads = width // HD
    base, positions = places(rows)
    last_position = jnp.zeros((8, LANES), jnp.int32) + (base + rows - 1)

    def one(d, starts):
        first = spans_ref[0, d]
        return tuple(
            jnp.where(at >= first, jnp.maximum(start, first), start)
            for start, at in zip(starts, (positions, last_position))
        )

    docs = spans_ref.shape[1]
    nothing = (jnp.zeros_like(positions), jnp.zeros_like(last_position))
    starts_ref[...], last_ref[...] = lax.fori_loop(0, docs, one, nothing, unroll=docs <= 16)
    r = lax.broadcasted_iota(jnp.int32, (rows, rows), 0)
    c = lax.broadcasted_iota(jnp.int32, (rows, rows), 1)
    upper = jnp.where(r <= c, 1.0, 0.0).astype(BF16)
    across = sum(dot(part, upper, ((1,), (0,))) for part in split3(decay_ref[...]))
    across_ref[...] = across
    head = lax.broadcasted_iota(jnp.int32, (heads, width), 0)
    lane = lax.broadcasted_iota(jnp.int32, (heads, width), 1)
    spread = jnp.where((lane >= head * HD) & (lane < (head + 1) * HD), 1.0, 0.0).astype(BF16)
    cum_ref[...] = sum(dot(part, spread, ((0,), (0,))) for part in split3(across))


def key_bias(starts_ref, rows, keys, behind):
    base, positions = places(rows)
    key = base - behind + lax.broadcasted_iota(jnp.int32, (rows, keys), 1)
    seen = (key >= wide(starts_ref[...], keys)) & (key <= wide(positions, keys))
    return jnp.where(seen, 0.0, NEG)


def state_kernel(last_ref, cum_ref, k_ref, v_ref, pack_ref, state_ref, dec_ref):
    rows, width = k_ref.shape
    base, positions = places(rows)
    start = last_ref[0:1, :]
    inside = positions >= start
    for h in range(width // HD):
        cols = slice(h * HD, (h + 1) * HD)
        mine = cum_ref[:, cols]
        last = mine[rows - 1 : rows, :]
        tail = jnp.where(inside, jnp.exp(jnp.minimum(last - mine, 0.0)), 0.0)
        tail_key = (k_ref[:, cols].astype(F32) * tail).astype(BF16)
        state = dot(tail_key, v_ref[:, cols], ((0,), (0,)))
        state_ref[:, cols] = state
        pack_ref[0:HD, cols] = state.astype(BF16)
        decay = jnp.broadcast_to(jnp.where(start < base, jnp.exp(last), 0.0), (8, HD))
        dec_ref[:, cols] = decay
        high = decay.astype(BF16).astype(F32)
        pack_ref[HD:, cols] = jnp.concatenate([high, decay - high], axis=0).astype(BF16)


def pick_kernel(there_ref, own_ref, out_ref):
    odd = lax.rem(lax.axis_index("seq"), 2) == 1

    @pl.when(odd)
    def _():
        out_ref[...] = there_ref[...]

    @pl.when(jnp.logical_not(odd))
    def _():
        out_ref[...] = own_ref[...]


def decays_of(pack_ref):
    return pack_ref[HD : HD + 1, :].astype(F32) + pack_ref[HD + 8 : HD + 9, :].astype(F32)


def pair_kernel(state_ref, dec_ref, other_ref, far_ref, k_ref, out_ref):
    reach = out_ref.shape[0] - HD
    odd = lax.rem(lax.axis_index("seq"), 2) == 1
    other, other_decay = other_ref[0:HD, :].astype(F32), decays_of(other_ref)
    own, own_decay = state_ref[...], dec_ref[0:1, :]

    @pl.when(odd)
    def _():
        out_ref[0:HD, :] = (own + own_decay * other).astype(BF16)

    @pl.when(jnp.logical_not(odd))
    def _():
        first = own + own_decay * far_ref[...].astype(F32)
        out_ref[0:HD, :] = (other + other_decay * first).astype(BF16)

    out_ref[HD:, :] = k_ref[k_ref.shape[0] - reach :, :]


def first_kernel(a_ref, out_ref):
    out_ref[...] = a_ref[0 : out_ref.shape[0], :]


def nearest_kernel(v_ref, out_ref):
    out_ref[...] = v_ref[v_ref.shape[0] - out_ref.shape[0] :, :]


def inner_kernel(
    starts_ref, q_ref, k_ref, v_ref, gate_ref, gain_ref, cum_ref, across_ref, inner_ref, scale_ref
):
    rows, width = k_ref.shape
    allowed = key_bias(starts_ref, rows, rows, 0) == 0.0
    for h in range(width // HD):
        cols = slice(h * HD, (h + 1) * HD)
        decayed = jnp.exp(jnp.minimum(wide(cum_ref[:, cols], rows) - across_ref[h : h + 1, :], 0.0))
        scores = dot(q_ref[:, cols], k_ref[:, cols], ((1,), (1,)))
        weights = jnp.where(allowed, scores * decayed, 0.0).astype(BF16)
        inner_ref[:, cols] = dot(weights, v_ref[:, cols], ((1,), (0,)))
        scale_ref[:, cols] = gain_ref[:, cols] * jax.nn.sigmoid(gate_ref[:, cols].astype(F32))


def cross_kernel(
    starts_ref, q_ref, cum_ref, inner_ref, other_ref, two_ref, mixture_ref, sq_ref
):
    rows, width = q_ref.shape
    base, _ = places(rows)
    enters = starts_ref[...] < base
    odd = lax.rem(lax.axis_index("seq"), 2) == 1
    kept = jnp.where(odd, 1.0, 0.0)
    passed = jnp.where(odd, decays_of(other_ref), 1.0)
    squares = jnp.zeros((rows, HD), F32)
    for h in range(width // HD):
        cols = slice(h * HD, (h + 1) * HD)
        carried = (
            kept * other_ref[0:HD, cols].astype(F32)
            + passed[:, cols] * two_ref[0:HD, cols].astype(F32)
        )
        cross = dot(q_ref[:, cols], carried.astype(BF16), ((1,), (0,)))
        mixture = inner_ref[:, cols] + cross * jnp.where(enters, jnp.exp(cum_ref[:, cols]), 0.0)
        squares = squares + mixture * mixture
        mixture_ref[:, cols] = mixture
    ones = jnp.ones((8, HD), BF16)
    sq_ref[...] = sum(dot(ones, part, ((1,), (1,))) for part in split3(squares))


def with_ones(v):
    return jnp.concatenate([v, jnp.ones_like(v)], axis=1)


def top_of(s):
    return jnp.broadcast_to(jnp.max(s, axis=1, keepdims=True), (s.shape[0], LANES))


def soft_own_kernel(starts_ref, q_ref, k_ref, v_ref, sums_ref, m_ref):
    rows, width = q_ref.shape
    bias = key_bias(starts_ref, rows, rows, 0)
    for h in range(width // HD):
        cols = slice(h * HD, (h + 1) * HD)
        s = dot(q_ref[:, cols], k_ref[:, cols], ((1,), (1,))) * SOFT_SCALE + bias
        m = top_of(s)
        m_ref[:, cols] = m
        p = jnp.exp2(s - wide(m, rows)).astype(BF16)
        sums_ref[:, 2 * h * HD : 2 * (h + 1) * HD] = dot(p, with_ones(v_ref[:, cols]), ((1,), (0,)))


def soft_grow_kernel(back, starts_ref, q_ref, k_ref, v_ref, sums0_ref, m0_ref, sums_ref, m_ref):
    rows, width = q_ref.shape
    keys = k_ref.shape[0]
    bias = key_bias(starts_ref, rows, keys, back * rows)
    for h in range(width // HD):
        cols = slice(h * HD, (h + 1) * HD)
        both = slice(2 * h * HD, 2 * (h + 1) * HD)
        m_old = m0_ref[:, cols]
        s = dot(q_ref[:, cols], k_ref[:, cols], ((1,), (1,))) * SOFT_SCALE + bias
        m = jnp.maximum(m_old, top_of(s))
        m_ref[:, cols] = m
        p = jnp.exp2(s - wide(m, keys)).astype(BF16)
        sums_ref[:, both] = sums0_ref[:, both] * wide(jnp.exp2(m_old - m), 2 * HD) + dot(
            p, with_ones(v_ref[:, cols]), ((1,), (0,))
        )


def soft_weigh_kernel(back, starts_ref, q_ref, k_ref, sums_ref, m_ref, p_ref, acc_ref, inv_ref):
    rows, width = q_ref.shape
    keys = k_ref.shape[0] - HD
    bias = key_bias(starts_ref, rows, keys, (back - 1) * rows + keys)
    ones = jnp.ones((keys, HD), BF16)
    for h in range(width // HD):
        cols = slice(h * HD, (h + 1) * HD)
        m_old = m_ref[:, cols]
        s = dot(q_ref[:, cols], k_ref[HD:, cols], ((1,), (1,))) * SOFT_SCALE + bias
        m = jnp.maximum(m_old, top_of(s))
        p = jnp.exp2(s - wide(m, keys)).astype(BF16)
        shrink = jnp.exp2(m_old - m)
        weight = sums_ref[:, (2 * h + 1) * HD : (2 * h + 2) * HD] * shrink + dot(
            p, ones, ((1,), (0,))
        )
        inv = 1.0 / weight
        p_ref[:, h * keys : (h + 1) * keys] = p
        acc_ref[:, cols] = sums_ref[:, 2 * h * HD : (2 * h + 1) * HD] * (shrink * inv)
        inv_ref[:, cols] = inv


def soft_last_kernel(p_ref, v_ref, acc_ref, inv_ref, soft_ref):
    keys = v_ref.shape[0]
    for h in range(acc_ref.shape[1] // HD):
        cols = slice(h * HD, (h + 1) * HD)
        more = dot(p_ref[:, h * keys : (h + 1) * keys], v_ref[:, cols], ((1,), (0,)))
        soft_ref[:, cols] = (acc_ref[:, cols] + more * inv_ref[:, cols]).astype(BF16)


def norm_kernel(mixture_ref, scale_ref, *refs):
    *parts, lin_ref = refs
    rows, width = lin_ref.shape
    total = jnp.transpose(sum(part[...] for part in parts))[:, 0:1]
    norm = jnp.broadcast_to(lax.rsqrt(total / (HALF_MODEL_HEADS * HD) + 1e-06), (rows, HD))
    for h in range(width // HD):
        cols = slice(h * HD, (h + 1) * HD)
        lin_ref[:, cols] = (mixture_ref[:, cols] * norm * scale_ref[:, cols]).astype(BF16)


SMEM = pl.BlockSpec(memory_space=pltpu.SMEM)
VMEM = pl.BlockSpec(memory_space=pltpu.VMEM)


def call(kernel, name, out_shape, *arrays, smem=0):
    return pl.pallas_call(
        kernel,
        name=name,
        out_shape=out_shape,
        in_specs=[SMEM] * smem + [VMEM] * (len(arrays) - smem),
        out_specs=jax.tree.map(lambda _: VMEM, out_shape),
        compiler_params=pltpu.CompilerParams(vmem_limit_bytes=VMEM_LIMIT),
    )(*arrays)


def program(
    reach,
    lin_query,
    lin_key,
    lin_value,
    log_decay,
    gate_logits,
    norm_gain,
    soft_query,
    soft_key,
    soft_value,
    doc_spans,
):
    rows, width = lin_query.shape
    heads = width // HD
    devices = lax.axis_size("seq")
    shape = jax.ShapeDtypeStruct

    def ahead(array, by, step=1):
        return lax.ppermute(
            array, "seq", [(i, i + by) for i in range(0, devices - by, step)]
        )

    def swap(array):
        return lax.ppermute(array, "seq", [(i, i ^ 1) for i in range(devices)])

    def everywhere(array):
        count = lax.axis_size("head")
        paired = count & (count - 1) == 0
        return [array] + [
            lax.ppermute(
                array, "head", [(i, i ^ by if paired else (i + by) % count) for i in range(count)]
            )
            for by in range(1, count)
        ]

    together = lax.optimization_barrier
    sums = (shape((rows, 2 * width), F32), shape((rows, width), F32))
    half = shape((rows, width), BF16)

    starts, last_start, cumulative, across = call(
        prep_kernel,
        "prep",
        (
            shape((rows, LANES), jnp.int32),
            shape((8, LANES), jnp.int32),
            shape((rows, width), F32),
            shape((heads, rows), F32),
        ),
        doc_spans.T, log_decay.T, smem=1,
    )
    k2 = ahead(soft_key, 2)
    pack, state, decay = call(
        state_kernel,
        "state",
        (shape((HD + 16, width), BF16), shape((HD, width), F32), shape((8, width), F32)),
        last_start, cumulative, lin_key, lin_value,
    )
    other = swap(pack)
    own_value, pack = together((soft_value, pack))
    v2 = ahead(own_value, 2)
    soft = call(soft_own_kernel, "soft_own", sums, starts, soft_query, soft_key, soft_value)
    own_key, top = together((soft_key, soft[1]))
    soft = (soft[0], top)
    k1 = swap(call(pick_kernel, "pick_k", half, k2, own_key))
    far = ahead(call(first_kernel, "states", shape((HD, width), BF16), other), 2, 2)
    v1 = swap(call(pick_kernel, "pick_v", half, v2, soft_value))
    pair = call(
        pair_kernel, "pair", shape((HD + reach, width), BF16), state, decay, other, far, k1
    )
    two = ahead(pair, 2)
    soft = call(
        functools.partial(soft_grow_kernel, 2), "soft_2", sums, starts, soft_query, k2, v2, *soft
    )
    inner, scale = call(
        inner_kernel, "inner", (shape((rows, width), F32), shape((rows, width), F32)),
        starts, lin_query, lin_key, lin_value, gate_logits, norm_gain.reshape(1, width),
        cumulative, across,
    )
    v1, top, inner = together((v1, soft[1], inner))
    soft = (soft[0], top)
    v3 = ahead(call(nearest_kernel, "nearest", shape((reach, width), BF16), v1), 2)
    soft = call(
        functools.partial(soft_grow_kernel, 1), "soft_1", sums, starts, soft_query, k1, v1, *soft
    )
    two, top = together((two, soft[1]))
    soft = (soft[0], top)
    mixture, squares = call(
        cross_kernel, "cross", (shape((rows, width), F32), shape((8, rows), F32)),
        starts, lin_query, cumulative, inner, other, two,
    )
    parts = everywhere(squares)
    weights, acc, inv = call(
        functools.partial(soft_weigh_kernel, SPAN), "soft_weigh",
        (
            shape((rows, heads * reach), BF16), shape((rows, width), F32),
            shape((rows, width), F32),
        ),
        starts, soft_query, two, *soft,
    )
    soft_out = call(soft_last_kernel, "soft_last", half, weights, v3, acc, inv)
    lin_out = call(norm_kernel, "norm", half, mixture, scale, *parts)
    return (lin_out, soft_out)


def shards(
    lin_query,
    lin_key,
    lin_value,
    log_decay,
    gate_logits,
    norm_gain,
    soft_query,
    soft_key,
    soft_value,
    doc_ids,
    doc_spans,
):
    rows = lin_query.shape[0]
    reach = rows // 2
    firsts, lasts = doc_spans[:, 0], doc_spans[:, 1] - 1
    farthest = jnp.max(lasts - lax.rem(lasts, jnp.int32(rows)) - firsts)
    return lax.cond(
        farthest <= (SPAN - 1) * rows + reach,
        functools.partial(program, reach),
        functools.partial(program, rows),
        lin_query, lin_key, lin_value, log_decay, gate_logits, norm_gain, soft_query, soft_key,
        soft_value, doc_spans,
    )


def solution(mesh):
    in_specs = (
        P("seq", "head"),
        P("seq", "head"),
        P("seq", "head"),
        P("seq", "head"),
        P("seq", "head"),
        P("head"),
        P("seq", "head"),
        P("seq", "head"),
        P("seq", "head"),
        P("seq"),
        P(),
    )
    out_specs = (P("seq", "head"), P("seq", "head"))
    return jax.shard_map(shards, mesh=mesh, in_specs=in_specs, out_specs=out_specs, check_vma=False)
```

```python
import functools

import jax
import jax.numpy as jnp
from jax import lax
from jax.experimental import pallas as pl
from jax.experimental.pallas import tpu as pltpu
from jax.sharding import PartitionSpec as P

HALF_MODEL_HEADS = 32
HD = 128
SPAN = 3
LANES = 128
NEG = -1e30
SOFT_SCALE = HD ** (-0.5) * 1.4426950408889634
F32 = jnp.float32
BF16 = jnp.bfloat16
VMEM_LIMIT = 6 * 1024 * 1024


def dot(a, b, dims):
    return lax.dot_general(a, b, (dims, ((), ())), preferred_element_type=F32)


def wide(column, width):
    return jnp.concatenate([column] * (width // LANES), axis=1)


def split3(x):
    high = x.astype(BF16)
    rest = x - high.astype(F32)
    middle = rest.astype(BF16)
    return high, middle, (rest - middle.astype(F32)).astype(BF16)


def places(rows):
    base = lax.axis_index("seq") * rows
    return base, base + lax.broadcasted_iota(jnp.int32, (rows, LANES), 0)


def prep_kernel(spans_ref, decay_ref, starts_ref, last_ref, cum_ref, across_ref):
    rows, width = cum_ref.shape
    heads = width // HD
    base, positions = places(rows)
    last_position = jnp.zeros((8, LANES), jnp.int32) + (base + rows - 1)

    def one(d, starts):
        first = spans_ref[0, d]
        return tuple(
            jnp.where(at >= first, jnp.maximum(start, first), start)
            for start, at in zip(starts, (positions, last_position))
        )

    docs = spans_ref.shape[1]
    nothing = (jnp.zeros_like(positions), jnp.zeros_like(last_position))
    starts_ref[...], last_ref[...] = lax.fori_loop(0, docs, one, nothing, unroll=docs <= 16)
    r = lax.broadcasted_iota(jnp.int32, (rows, rows), 0)
    c = lax.broadcasted_iota(jnp.int32, (rows, rows), 1)
    upper = jnp.where(r <= c, 1.0, 0.0).astype(BF16)
    across = sum(dot(part, upper, ((1,), (0,))) for part in split3(decay_ref[...]))
    across_ref[...] = across
    head = lax.broadcasted_iota(jnp.int32, (heads, width), 0)
    lane = lax.broadcasted_iota(jnp.int32, (heads, width), 1)
    spread = jnp.where((lane >= head * HD) & (lane < (head + 1) * HD), 1.0, 0.0).astype(BF16)
    cum_ref[...] = sum(dot(part, spread, ((0,), (0,))) for part in split3(across))


def key_bias(starts_ref, rows, keys, behind):
    base, positions = places(rows)
    key = base - behind + lax.broadcasted_iota(jnp.int32, (rows, keys), 1)
    seen = (key >= wide(starts_ref[...], keys)) & (key <= wide(positions, keys))
    return jnp.where(seen, 0.0, NEG)


def state_kernel(last_ref, cum_ref, k_ref, v_ref, pack_ref, state_ref, dec_ref):
    rows, width = k_ref.shape
    base, positions = places(rows)
    start = last_ref[0:1, :]
    inside = positions >= start
    for h in range(width // HD):
        cols = slice(h * HD, (h + 1) * HD)
        mine = cum_ref[:, cols]
        last = mine[rows - 1 : rows, :]
        tail = jnp.where(inside, jnp.exp(jnp.minimum(last - mine, 0.0)), 0.0)
        tail_key = (k_ref[:, cols].astype(F32) * tail).astype(BF16)
        state = dot(tail_key, v_ref[:, cols], ((0,), (0,)))
        state_ref[:, cols] = state
        pack_ref[0:HD, cols] = state.astype(BF16)
        decay = jnp.broadcast_to(jnp.where(start < base, jnp.exp(last), 0.0), (8, HD))
        dec_ref[:, cols] = decay
        high = decay.astype(BF16).astype(F32)
        pack_ref[HD:, cols] = jnp.concatenate([high, decay - high], axis=0).astype(BF16)


def pick_kernel(there_ref, own_ref, out_ref):
    odd = lax.rem(lax.axis_index("seq"), 2) == 1

    @pl.when(odd)
    def _():
        out_ref[...] = there_ref[...]

    @pl.when(jnp.logical_not(odd))
    def _():
        out_ref[...] = own_ref[...]


def decays_of(pack_ref):
    return pack_ref[HD : HD + 1, :].astype(F32) + pack_ref[HD + 8 : HD + 9, :].astype(F32)


def pair_kernel(state_ref, dec_ref, other_ref, far_ref, k_ref, out_ref):
    reach = out_ref.shape[0] - HD
    odd = lax.rem(lax.axis_index("seq"), 2) == 1
    other, other_decay = other_ref[0:HD, :].astype(F32), decays_of(other_ref)
    own, own_decay = state_ref[...], dec_ref[0:1, :]

    @pl.when(odd)
    def _():
        out_ref[0:HD, :] = (own + own_decay * other).astype(BF16)

    @pl.when(jnp.logical_not(odd))
    def _():
        first = own + own_decay * far_ref[...].astype(F32)
        out_ref[0:HD, :] = (other + other_decay * first).astype(BF16)

    out_ref[HD:, :] = k_ref[k_ref.shape[0] - reach :, :]


def first_kernel(a_ref, out_ref):
    out_ref[...] = a_ref[0 : out_ref.shape[0], :]


def nearest_kernel(v_ref, out_ref):
    out_ref[...] = v_ref[v_ref.shape[0] - out_ref.shape[0] :, :]


def inner_kernel(
    starts_ref, q_ref, k_ref, v_ref, gate_ref, gain_ref, cum_ref, across_ref, inner_ref, scale_ref
):
    rows, width = k_ref.shape
    allowed = key_bias(starts_ref, rows, rows, 0) == 0.0
    for h in range(width // HD):
        cols = slice(h * HD, (h + 1) * HD)
        decayed = jnp.exp(jnp.minimum(wide(cum_ref[:, cols], rows) - across_ref[h : h + 1, :], 0.0))
        scores = dot(q_ref[:, cols], k_ref[:, cols], ((1,), (1,)))
        weights = jnp.where(allowed, scores * decayed, 0.0).astype(BF16)
        inner_ref[:, cols] = dot(weights, v_ref[:, cols], ((1,), (0,)))
        scale_ref[:, cols] = gain_ref[:, cols] * jax.nn.sigmoid(gate_ref[:, cols].astype(F32))


def cross_kernel(
    starts_ref, q_ref, cum_ref, inner_ref, other_ref, two_ref, mixture_ref, sq_ref
):
    rows, width = q_ref.shape
    base, _ = places(rows)
    enters = starts_ref[...] < base
    odd = lax.rem(lax.axis_index("seq"), 2) == 1
    kept = jnp.where(odd, 1.0, 0.0)
    passed = jnp.where(odd, decays_of(other_ref), 1.0)
    squares = jnp.zeros((rows, HD), F32)
    for h in range(width // HD):
        cols = slice(h * HD, (h + 1) * HD)
        carried = (
            kept * other_ref[0:HD, cols].astype(F32)
            + passed[:, cols] * two_ref[0:HD, cols].astype(F32)
        )
        cross = dot(q_ref[:, cols], carried.astype(BF16), ((1,), (0,)))
        mixture = inner_ref[:, cols] + cross * jnp.where(enters, jnp.exp(cum_ref[:, cols]), 0.0)
        squares = squares + mixture * mixture
        mixture_ref[:, cols] = mixture
    ones = jnp.ones((8, HD), BF16)
    sq_ref[...] = sum(dot(ones, part, ((1,), (1,))) for part in split3(squares))


def with_ones(v):
    return jnp.concatenate([v, jnp.ones_like(v)], axis=1)


def top_of(s):
    return jnp.broadcast_to(jnp.max(s, axis=1, keepdims=True), (s.shape[0], LANES))


def soft_own_kernel(starts_ref, q_ref, k_ref, v_ref, sums_ref, m_ref):
    rows, width = q_ref.shape
    bias = key_bias(starts_ref, rows, rows, 0)
    for h in range(width // HD):
        cols = slice(h * HD, (h + 1) * HD)
        s = dot(q_ref[:, cols], k_ref[:, cols], ((1,), (1,))) * SOFT_SCALE + bias
        m = top_of(s)
        m_ref[:, cols] = m
        p = jnp.exp2(s - wide(m, rows)).astype(BF16)
        sums_ref[:, 2 * h * HD : 2 * (h + 1) * HD] = dot(p, with_ones(v_ref[:, cols]), ((1,), (0,)))


def soft_grow_kernel(back, starts_ref, q_ref, k_ref, v_ref, sums0_ref, m0_ref, sums_ref, m_ref):
    rows, width = q_ref.shape
    keys = k_ref.shape[0]
    bias = key_bias(starts_ref, rows, keys, back * rows)
    for h in range(width // HD):
        cols = slice(h * HD, (h + 1) * HD)
        both = slice(2 * h * HD, 2 * (h + 1) * HD)
        m_old = m0_ref[:, cols]
        s = dot(q_ref[:, cols], k_ref[:, cols], ((1,), (1,))) * SOFT_SCALE + bias
        m = jnp.maximum(m_old, top_of(s))
        m_ref[:, cols] = m
        p = jnp.exp2(s - wide(m, keys)).astype(BF16)
        sums_ref[:, both] = sums0_ref[:, both] * wide(jnp.exp2(m_old - m), 2 * HD) + dot(
            p, with_ones(v_ref[:, cols]), ((1,), (0,))
        )


def soft_end_kernel(starts_ref, q_ref, k_ref, v_ref, sums_ref, m_ref, soft_ref):
    rows, width = q_ref.shape
    keys = v_ref.shape[0]
    bias = key_bias(starts_ref, rows, keys, (SPAN - 1) * rows + keys)
    for h in range(width // HD):
        cols = slice(h * HD, (h + 1) * HD)
        both = slice(2 * h * HD, 2 * (h + 1) * HD)
        m_old = m_ref[:, cols]
        s = dot(q_ref[:, cols], k_ref[HD:, cols], ((1,), (1,))) * SOFT_SCALE + bias
        m = jnp.maximum(m_old, top_of(s))
        p = jnp.exp2(s - wide(m, keys)).astype(BF16)
        total = sums_ref[:, both] * wide(jnp.exp2(m_old - m), 2 * HD) + dot(
            p, with_ones(v_ref[:, cols]), ((1,), (0,))
        )
        soft_ref[:, cols] = (total[:, :HD] / total[:, HD:]).astype(BF16)


def norm_kernel(mixture_ref, scale_ref, *refs):
    *parts, lin_ref = refs
    rows, width = lin_ref.shape
    total = jnp.transpose(sum(part[...] for part in parts))[:, 0:1]
    norm = jnp.broadcast_to(lax.rsqrt(total / (HALF_MODEL_HEADS * HD) + 1e-06), (rows, HD))
    for h in range(width // HD):
        cols = slice(h * HD, (h + 1) * HD)
        lin_ref[:, cols] = (mixture_ref[:, cols] * norm * scale_ref[:, cols]).astype(BF16)


SMEM = pl.BlockSpec(memory_space=pltpu.SMEM)
VMEM = pl.BlockSpec(memory_space=pltpu.VMEM)


def call(kernel, name, out_shape, *arrays, smem=0):
    return pl.pallas_call(
        kernel,
        name=name,
        out_shape=out_shape,
        in_specs=[SMEM] * smem + [VMEM] * (len(arrays) - smem),
        out_specs=jax.tree.map(lambda _: VMEM, out_shape),
        compiler_params=pltpu.CompilerParams(vmem_limit_bytes=VMEM_LIMIT),
    )(*arrays)


def program(
    reach,
    lin_query,
    lin_key,
    lin_value,
    log_decay,
    gate_logits,
    norm_gain,
    soft_query,
    soft_key,
    soft_value,
    doc_spans,
):
    rows, width = lin_query.shape
    heads = width // HD
    devices = lax.axis_size("seq")
    shape = jax.ShapeDtypeStruct

    def ahead(array, by, step=1):
        return lax.ppermute(
            array, "seq", [(i, i + by) for i in range(0, devices - by, step)]
        )

    def swap(array):
        return lax.ppermute(array, "seq", [(i, i ^ 1) for i in range(devices)])

    def everywhere(array):
        count = lax.axis_size("head")
        paired = count & (count - 1) == 0
        return [array] + [
            lax.ppermute(
                array, "head", [(i, i ^ by if paired else (i + by) % count) for i in range(count)]
            )
            for by in range(1, count)
        ]

    together = lax.optimization_barrier
    sums = (shape((rows, 2 * width), F32), shape((rows, width), F32))
    half = shape((rows, width), BF16)

    starts, last_start, cumulative, across = call(
        prep_kernel,
        "prep",
        (
            shape((rows, LANES), jnp.int32),
            shape((8, LANES), jnp.int32),
            shape((rows, width), F32),
            shape((heads, rows), F32),
        ),
        doc_spans.T, log_decay.T, smem=1,
    )
    k2 = ahead(soft_key, 2)
    pack, state, decay = call(
        state_kernel,
        "state",
        (shape((HD + 16, width), BF16), shape((HD, width), F32), shape((8, width), F32)),
        last_start, cumulative, lin_key, lin_value,
    )
    other = swap(pack)
    own_value, pack = together((soft_value, pack))
    v2 = ahead(own_value, 2)
    soft = call(soft_own_kernel, "soft_own", sums, starts, soft_query, soft_key, soft_value)
    own_key, top = together((soft_key, soft[1]))
    soft = (soft[0], top)
    k1 = swap(call(pick_kernel, "pick_k", half, k2, own_key))
    far = ahead(call(first_kernel, "states", shape((HD, width), BF16), other), 2, 2)
    v1 = swap(call(pick_kernel, "pick_v", half, v2, soft_value))
    pair = call(
        pair_kernel, "pair", shape((HD + reach, width), BF16), state, decay, other, far, k1
    )
    two = ahead(pair, 2)
    soft = call(
        functools.partial(soft_grow_kernel, 2), "soft_2", sums, starts, soft_query, k2, v2, *soft
    )
    inner, scale = call(
        inner_kernel, "inner", (shape((rows, width), F32), shape((rows, width), F32)),
        starts, lin_query, lin_key, lin_value, gate_logits, norm_gain.reshape(1, width),
        cumulative, across,
    )
    v1, top, inner = together((v1, soft[1], inner))
    soft = (soft[0], top)
    v3 = ahead(call(nearest_kernel, "nearest", shape((reach, width), BF16), v1), 2)
    soft = call(
        functools.partial(soft_grow_kernel, 1), "soft_1", sums, starts, soft_query, k1, v1, *soft
    )
    two, top = together((two, soft[1]))
    soft = (soft[0], top)
    mixture, squares = call(
        cross_kernel, "cross", (shape((rows, width), F32), shape((8, rows), F32)),
        starts, lin_query, cumulative, inner, other, two,
    )
    parts = everywhere(squares)
    soft_out = call(soft_end_kernel, "soft_end", half, starts, soft_query, two, v3, *soft)
    lin_out = call(norm_kernel, "norm", half, mixture, scale, *parts)
    return (lin_out, soft_out)


def shards(
    lin_query,
    lin_key,
    lin_value,
    log_decay,
    gate_logits,
    norm_gain,
    soft_query,
    soft_key,
    soft_value,
    doc_ids,
    doc_spans,
):
    rows = lin_query.shape[0]
    reach = rows // 2
    firsts, lasts = doc_spans[:, 0], doc_spans[:, 1] - 1
    farthest = jnp.max(lasts - lax.rem(lasts, jnp.int32(rows)) - firsts)
    return lax.cond(
        farthest <= (SPAN - 1) * rows + reach,
        functools.partial(program, reach),
        functools.partial(program, rows),
        lin_query, lin_key, lin_value, log_decay, gate_logits, norm_gain, soft_query, soft_key,
        soft_value, doc_spans,
    )


def solution(mesh):
    in_specs = (
        P("seq", "head"),
        P("seq", "head"),
        P("seq", "head"),
        P("seq", "head"),
        P("seq", "head"),
        P("head"),
        P("seq", "head"),
        P("seq", "head"),
        P("seq", "head"),
        P("seq"),
        P(),
    )
    out_specs = (P("seq", "head"), P("seq", "head"))
    return jax.shard_map(shards, mesh=mesh, in_specs=in_specs, out_specs=out_specs, check_vma=False)
```
